32 devices in a mesh: mem: 16 (over z, y, x), patch: 2 (over core).
Axes of the slice: x: 2, y: 2, z: 4, core: 2. Of those that a mesh axis runs over, the one named last changes fastest.
Arguments:
- state: bfloat16 [3, 1024, 8192], P(None, 'mem', 'patch'), may hold values from -6 to 6
- obs_noise: bfloat16 [1024, 8192], P('mem', 'patch'), may hold values from -6 to 6
- obs_values: float32 [2, 4096], P('patch', 'mem'), may hold values from -6 to 6
- obs_weights: bfloat16 [2, 32, 128, 128], P('patch', 'mem'), may hold values from -1 to 1
- tapers: float32 [8, 128, 128], replicated, may hold values from 0.2 to 1
- pair_source: int32 [2, 32, 4], P('patch', 'mem'), may hold values from 0 to 31, as said below
- pair_taper: int32 [2, 32, 4], P('patch', 'mem'), may hold values from 0 to 7
Outputs:
- analysis: bfloat16 [3, 1024, 8192], P(None, 'mem', 'patch')
The draws below stay inside these ranges and needn't reach their ends.
Inputs may be any that keep to these rules, and one draw needn't show every extreme that they name: `pair_source`: each listed source lies in the same patch within 2 blocks of its target block; positions beyond the patch's ends are moved to its first or last block.
All inputs are finite; a program needn't handle non-finite values.
Results may differ from the reference program's by a relative error of at most 0.0058.
Values may be sent and summed in bfloat16 or wider, within the bound.
A program may use at most 64 MiB of HBM per device.

```python
import jax
import jax.numpy as jnp
from jax import lax

MEMBERS = 1024
VARIABLES = 3
BLOCK_CELLS = 128
RADIUS = 2
PAIRS = 4
TAPERS = 8
PATCHES = 2
PATCH_BLOCKS = 32
PATCH_CELLS = 4096
TOTAL_CELLS = 8192


def draw_obs_weights(key, part):
    first_key, second_key = jax.random.split(jax.random.fold_in(key, 17))
    shape = (PATCHES, PATCH_BLOCKS, BLOCK_CELLS, BLOCK_CELLS)
    diagonal = jnp.exp(jax.random.uniform(first_key, shape[:3], jnp.float32, jnp.log(0.3), 0.0))
    spread = jax.random.normal(second_key, shape, jnp.float32)
    offdiag = jnp.clip(spread * 0.5 / jnp.sqrt(1.0 * BLOCK_CELLS), -0.3, 0.3)
    unit = jnp.eye(BLOCK_CELLS, dtype=jnp.float32)
    weights = offdiag * (1.0 - unit) + unit * diagonal[..., None]
    return weights.astype(jnp.bfloat16)


def draw_pair_source(key, part):
    width = 2 * RADIUS + 1
    scores = jax.random.randint(jax.random.fold_in(key, 29), (PATCHES, PATCH_BLOCKS, width), 0, 4096)
    scores = scores * 8 + jnp.arange(width, dtype=jnp.int32)
    order = jnp.argsort(scores, axis=-1, stable=True)[..., :PAIRS].astype(jnp.int32)
    target = jnp.arange(PATCH_BLOCKS, dtype=jnp.int32)[None, :, None]
    source = jnp.clip(target + order - RADIUS, 0, PATCH_BLOCKS - 1)
    return source.astype(jnp.int32)


def plant(drawn, own_key, smallest, high):
    extent = drawn.shape
    index_at = [jax.random.randint(jax.random.fold_in(own_key, axis), (), 0, extent[axis]) for axis in range(len(extent))]
    drawn = drawn.at[tuple(index_at)].set(smallest)
    longest = extent.index(max(extent))
    index_at[longest] = (index_at[longest] + 1) % extent[longest]
    return drawn.at[tuple(index_at)].set(high)


def shard_levels(own_key, shape, shards, least, top_value):
    loudness, own = 1.0, jax.random.fold_in(own_key, 6)
    for axis_at, parts in shards:
        heights = jnp.exp(jax.random.uniform(jax.random.fold_in(own, axis_at), (parts,), jnp.float32, least / len(shards), top_value / len(shards)))
        loudness = loudness * jnp.repeat(heights, shape[axis_at] // parts).reshape([-1 if axis == axis_at else 1 for axis in range(len(shape))])
    return loudness


def normal_values(own_key, dims, deviation, reach, cuts=(), held_as=jnp.bfloat16):
    entries = jax.random.normal(own_key, dims, jnp.float32) * deviation
    if len(cuts) > 0:
        entries = shard_levels(own_key, dims, cuts, -0.22, 0.18) * entries
    return jnp.clip(entries, min=-reach, max=reach).astype(held_as)


def setup_inputs(seed: int = 0) -> dict:
    arg_keys = jax.random.split(jax.random.key(seed), 8)
    state = normal_values(arg_keys[0], (VARIABLES, MEMBERS, TOTAL_CELLS), 1.0, 6.0, ((1, 16), (2, 2)))
    obs_noise = normal_values(arg_keys[1], (MEMBERS, TOTAL_CELLS), 1.0, 6.0, ((0, 16), (1, 2)))
    obs_values = normal_values(arg_keys[2], (PATCHES, PATCH_CELLS), 1.0, 6.0, ((0, 2), (1, 16)), jnp.float32)
    obs_weights = draw_obs_weights(jax.random.fold_in(arg_keys[7], 71), 0)
    tapers = jnp.clip(jax.random.uniform(arg_keys[4], (TAPERS, BLOCK_CELLS, BLOCK_CELLS), jnp.float32, 0.2, 1.0), 0.2, 1.0)
    pair_source = draw_pair_source(jax.random.fold_in(arg_keys[7], 71), 0)
    pair_taper = plant(jax.random.randint(arg_keys[6], (PATCHES, PATCH_BLOCKS, PAIRS), 0, TAPERS), jax.random.fold_in(arg_keys[6], 1), 0, TAPERS - 1).astype(jnp.int32)
    return {"state": state, "obs_noise": obs_noise, "obs_values": obs_values, "obs_weights": obs_weights, "tapers": tapers, "pair_source": pair_source, "pair_taper": pair_taper}


def reference(state, obs_noise, obs_values, obs_weights, tapers, pair_source, pair_taper):
    grid = state.reshape(VARIABLES, MEMBERS, PATCHES, PATCH_BLOCKS, BLOCK_CELLS).astype(jnp.float32)
    center = jnp.mean(grid, axis=1, keepdims=True)
    anomaly = (grid - center).astype(jnp.bfloat16)
    noise_grid = obs_noise.reshape(MEMBERS, PATCHES, PATCH_BLOCKS, BLOCK_CELLS).astype(jnp.float32)
    observed = obs_values.reshape(PATCHES, PATCH_BLOCKS, BLOCK_CELLS)
    innovation = (observed[None] + noise_grid - grid[0]).astype(jnp.bfloat16)
    weighted = jnp.einsum("pbcd,npbd->npbc", obs_weights.astype(jnp.float32),
                          innovation.astype(jnp.float32)).astype(jnp.bfloat16)

    def per_patch(patch):
        anom_patch = anomaly[:, :, patch]
        weight_patch = weighted[:, patch]
        source_patch = pair_source[patch]
        taper_patch = pair_taper[patch]

        def per_target(target):
            target_anom = anom_patch[:, :, target].astype(jnp.float32)
            total = jnp.zeros((VARIABLES, MEMBERS, BLOCK_CELLS), jnp.float32)
            for slot in range(PAIRS):
                source = source_patch[target, slot]
                source_anom = anom_patch[0, :, source].astype(jnp.float32)
                source_weight = weight_patch[:, source].astype(jnp.float32)
                taper = tapers[taper_patch[target, slot]]
                covariance = jnp.einsum("vnc,nd->vcd", target_anom, source_anom) / (MEMBERS - 1)
                localized = (taper * covariance).astype(jnp.bfloat16)
                total = total + jnp.einsum("nd,vcd->vnc", source_weight, localized.astype(jnp.float32))
            return total

        return lax.map(per_target, jnp.arange(PATCH_BLOCKS, dtype=jnp.int32))

    increment = lax.map(per_patch, jnp.arange(PATCHES, dtype=jnp.int32))
    increment = jnp.transpose(increment, (2, 3, 0, 1, 4)).reshape(VARIABLES, MEMBERS, TOTAL_CELLS)
    return (state.astype(jnp.float32) + increment).astype(jnp.bfloat16)
```

```python
import functools

import jax
import jax.numpy as jnp
from jax import lax
from jax.experimental import pallas as pl
from jax.experimental.pallas import tpu as pltpu
from jax.sharding import PartitionSpec as P

RADIUS = 2
MESH = pl.DeviceIdType.MESH


def seat_of(place, part, places):
    span = places // 4
    leg, step = place // span, place % span
    level = (leg + 1) // 2 % 2
    step = step + (leg % 2) * (span - 1 - 2 * step)
    spot = leg // 2 * span + step
    spot = spot + (part % 2) * (2 * span - 1 - 2 * spot)
    return level * 2 * span + spot


def place_of(seat, part, places):
    span = places // 4
    level, spot = seat // (2 * span), seat % (2 * span)
    spot = spot + (part % 2) * (2 * span - 1 - 2 * spot)
    side, step = spot // span, spot % span
    leg = level + side * (3 - 2 * level)
    step = step + (leg % 2) * (span - 1 - 2 * step)
    return leg * span + step


def kernel(
    n,
    state, noise, obs_values, obs_weights, tapers, pair_source, pair_taper,
    out,
    own_state, own_noise, innov, values, rin, guest_in, inn, anom, win_at, win_w, loc, taper_in, taper_t, outbuf,
    weights_in, source_in, choice_in,
    local_sem, values_send, values_recv, in_send, in_recv, guest_send, guest_recv, guest_local,
    inn_send, inn_recv, small_send, small_recv, halo_send, halo_recv, loc_send, loc_recv,
    out_send, out_recv, keep_sem,
):
    me = lax.axis_index("mem")
    part = lax.axis_index("patch")
    variables, rows, cells = state.shape
    places = n // 2
    leads_each = places // 2
    width = cells // places
    owned = cells // n
    blocks, size = obs_weights.shape[1], obs_weights.shape[2]
    per = width // size
    pairs = pair_source.shape[2]
    members = n * rows
    half, seat = me // places, me % places
    place = place_of(seat, part, places)
    leads = place // leads_each == half
    low, high = leads_each - 1, leads_each
    is_guest = jnp.logical_and(leads, jnp.logical_or(place == low, place == high))
    edge = RADIUS * size

    def device_of(side, where):
        return side * places + seat_of(where, part, places)

    def lead_of(where):
        return device_of(where // leads_each, where)

    def columns(where):
        return pl.ds(pl.multiple_of(where * width, width), width)

    barrier = pltpu.get_barrier_semaphore()

    def greet(k, _):
        peer = lax.rem(me + k, n)
        pl.semaphore_signal(barrier, inc=1, device_id=(peer, part), device_id_type=MESH)
        return 0

    lax.fori_loop(1, n, greet, 0)

    my_rows = pl.ds(pl.multiple_of(me * rows, rows), rows)
    seat_rows = pl.ds(pl.multiple_of(seat * rows, rows), rows)
    mine = columns(place)

    own_copies = [
        pltpu.make_async_copy(state.at[0], own_state, local_sem.at[variables]),
        pltpu.make_async_copy(noise, own_noise, local_sem.at[variables + 1]),
    ]
    for copy in own_copies:
        copy.start()
    taper_copy = pltpu.make_async_copy(tapers, taper_in, local_sem.at[variables + 2])
    taper_copy.start()
    my_values = values.at[:, pl.ds(pl.multiple_of(me * owned, owned), owned)]
    values_copy = pltpu.make_async_copy(obs_values, my_values, local_sem.at[variables + 3])
    values_copy.start()

    raw_local = [
        pltpu.make_async_copy(state.at[v, :, mine], rin.at[v, my_rows], local_sem.at[v]) for v in range(variables)
    ]

    @pl.when(leads)
    def _():
        for copy in raw_local:
            copy.start()

    pl.semaphore_wait(barrier, n - 1)

    def send_values(k, _):
        pltpu.make_async_remote_copy(
            src_ref=obs_values,
            dst_ref=my_values,
            send_sem=values_send,
            recv_sem=values_recv,
            device_id=(lax.rem(me + k, n), part),
            device_id_type=MESH,
        ).start()
        return 0

    lax.fori_loop(1, n, send_values, 0)

    def send_raw(v, side):
        def send(k, _):
            where = side * leads_each + lax.rem(seat + k, leads_each)
            peer = lead_of(where)

            @pl.when(peer != me)
            def _():
                pltpu.make_async_remote_copy(
                    src_ref=state.at[v, :, columns(where)],
                    dst_ref=rin.at[v, my_rows],
                    send_sem=in_send.at[v],
                    recv_sem=in_recv.at[v],
                    device_id=(peer, part),
                    device_id_type=MESH,
                ).start()

            return 0

        lax.fori_loop(0, leads_each, send, 0)

    def edge_of(host):
        start = high * width if host == low else high * width - edge
        return state.at[0, :, pl.ds(start, edge)]

    def send_guests():
        for host in (low, high):
            peer = lead_of(host)

            @pl.when(peer != me)
            def _():
                pltpu.make_async_remote_copy(
                    src_ref=edge_of(host),
                    dst_ref=guest_in.at[my_rows],
                    send_sem=guest_send,
                    recv_sem=guest_recv,
                    device_id=(peer, part),
                    device_id_type=MESH,
                ).start()

            @pl.when(peer == me)
            def _():
                pltpu.make_async_copy(edge_of(host), guest_in.at[my_rows], guest_local).start()

    send_raw(0, 1 - half)
    send_guests()
    send_raw(0, half)

    slot = me % 2
    keeper = me // 2
    small = [
        (obs_weights.at[0], weights_in),
        (pair_source.at[0], source_in),
        (pair_taper.at[0], choice_in),
    ]

    def small_remote(i, side):
        return pltpu.make_async_remote_copy(
            src_ref=small[i][0],
            dst_ref=small[i][1].at[slot],
            send_sem=small_send.at[i, side],
            recv_sem=small_recv.at[i, slot],
            device_id=(device_of(side, keeper), part),
            device_id_type=MESH,
        )

    for side in range(2):
        @pl.when(device_of(side, keeper) != me)
        def _():
            for i in range(len(small)):
                small_remote(i, side).start()

        @pl.when(device_of(side, keeper) == me)
        def _():
            for i in range(len(small)):
                pltpu.make_async_copy(small[i][0], small[i][1].at[slot], small_recv.at[i, slot]).start()

    def small_arrived():
        for i in range(len(small)):
            for s in range(2):
                here = small[i][1].at[s]
                pltpu.make_async_copy(here, here, small_recv.at[i, s]).wait()

    for copy in own_copies:
        copy.wait()
    values_copy.wait()
    others = values.at[:, pl.ds(0, (n - 1) * owned)]
    pltpu.make_async_copy(others, others, values_recv).wait()

    def innovate(p, _):
        here = columns(p)
        innov[:, here] = (
            values[:, here] + own_noise[:, here].astype(jnp.float32) - own_state[:, here].astype(jnp.float32)
        ).astype(jnp.bfloat16)
        return 0

    lax.fori_loop(0, places, innovate, 0)

    def send_innov(k, _):
        where = lax.rem(place + k, places)
        pltpu.make_async_remote_copy(
            src_ref=innov.at[:, columns(where)],
            dst_ref=inn.at[seat_rows],
            send_sem=inn_send,
            recv_sem=inn_recv,
            device_id=(device_of(half, where), part),
            device_id_type=MESH,
        ).start()
        return 0

    lax.fori_loop(1, places, send_innov, 0)
    inn_copy = pltpu.make_async_copy(innov.at[:, mine], inn.at[seat_rows], local_sem.at[variables + 4])
    inn_copy.start()
    send_raw(1, 1 - half)

    taper_copy.wait()

    def flip(k, _):
        taper_t[k] = taper_in[k].T * (1.0 / (members - 1))
        return 0

    lax.fori_loop(0, tapers.shape[0], flip, 0)

    remote_rows = pl.ds(0, (n - 1) * rows)

    def arrived(v):
        raw_local[v].wait()
        block = rin.at[v, remote_rows]
        pltpu.make_async_copy(block, block, in_recv.at[v]).wait()

    def centered(array):
        numbers = array.astype(jnp.float32)
        center = jnp.sum(numbers, axis=0, keepdims=True) * (1.0 / members)
        return (numbers - center).astype(jnp.bfloat16)

    def block_of(b):
        return pl.ds(pl.multiple_of(b * size, size), size)

    def exchange(window, index, before, after):
        left = pltpu.make_async_remote_copy(
            src_ref=window.at[pl.ds(RADIUS, RADIUS)],
            dst_ref=window.at[pl.ds(RADIUS + per, RADIUS)],
            send_sem=halo_send.at[index, 0],
            recv_sem=halo_recv.at[index, 0],
            device_id=(device_of(half, jnp.maximum(place - 1, 0)), part),
            device_id_type=MESH,
        )
        right = pltpu.make_async_remote_copy(
            src_ref=window.at[pl.ds(per, RADIUS)],
            dst_ref=window.at[pl.ds(0, RADIUS)],
            send_sem=halo_send.at[index, 1],
            recv_sem=halo_recv.at[index, 1],
            device_id=(device_of(half, jnp.minimum(place + 1, places - 1)), part),
            device_id_type=MESH,
        )

        def start():
            @pl.when(before)
            def _():
                left.start()

            @pl.when(after)
            def _():
                right.start()

        def landed():
            @pl.when(before)
            def _():
                left.wait_send()
                right.wait_recv()

            @pl.when(after)
            def _():
                right.wait_send()
                left.wait_recv()

        return start, landed

    at_start, at_landed = exchange(
        win_at,
        0,
        jnp.logical_and(leads, jnp.logical_and(place > 0, place != high)),
        jnp.logical_and(leads, jnp.logical_and(place < places - 1, place != low)),
    )
    w_start, w_landed = exchange(win_w, 1, place > 0, place < places - 1)

    @pl.when(leads)
    def _():
        arrived(0)

        def prepare(b, _):
            first = centered(rin[0, :, block_of(b)])
            anom[0, :, block_of(b)] = first
            win_at[RADIUS + b] = first.T
            return 0

        lax.fori_loop(0, per, prepare, 0)

    at_start()
    send_raw(1, half)
    send_raw(2, 1 - half)
    send_raw(2, half)
    for v in range(3, variables):
        send_raw(v, 1 - half)
        send_raw(v, half)

    small_arrived()
    inn_copy.wait()
    others_rows = inn.at[pl.ds(0, (places - 1) * rows)]
    pltpu.make_async_copy(others_rows, others_rows, inn_recv).wait()

    def weigh(b, _):
        win_w[RADIUS + b] = lax.dot_general(
            inn[:, block_of(b)],
            weights_in[b // blocks, b % blocks],
            (((1,), (1,)), ((), ())),
            preferred_element_type=jnp.float32,
        ).astype(jnp.bfloat16)
        return 0

    lax.fori_loop(0, per, weigh, 0)
    w_start()

    @pl.when(is_guest)
    def _():
        pltpu.make_async_copy(guest_in.at[my_rows], guest_in.at[my_rows], guest_local).wait()
        block = guest_in.at[remote_rows]
        pltpu.make_async_copy(block, block, guest_recv).wait()
        start = jnp.where(place == low, RADIUS + per, 0)
        for b in range(RADIUS):
            win_at[start + b] = centered(guest_in[:, b * size : (b + 1) * size]).T

    base = place * per - RADIUS

    def near(b, j):
        return jnp.clip(source_in[b // blocks, b % blocks, j] - base, 0, win_at.shape[0] - 1)

    def loc_copy(v, b):
        return pltpu.make_async_remote_copy(
            src_ref=loc.at[v, b],
            dst_ref=loc.at[v, b],
            send_sem=loc_send.at[v, b],
            recv_sem=loc_recv.at[v, b],
            device_id=(device_of(1 - half, place), part),
            device_id_type=MESH,
        )

    def localize(v):
        def step(b, _):
            for j in range(pairs):
                covariance = jnp.dot(
                    win_at[near(b, j)],
                    anom[v, :, block_of(b)],
                    preferred_element_type=jnp.float32,
                )
                loc[v, b, pl.ds(j * size, size), :] = (
                    covariance * taper_t[choice_in[b // blocks, b % blocks, j]]
                ).astype(jnp.bfloat16)
            loc_copy(v, b).start()
            return 0

        lax.fori_loop(0, per, step, 0)

    def center_all(v):
        def step(b, _):
            anom[v, :, block_of(b)] = centered(rin[v, :, block_of(b)])
            return 0

        lax.fori_loop(0, per, step, 0)

    def answer(v, b):
        weights = jnp.concatenate([win_w[near(b, j)] for j in range(pairs)], axis=1)
        increment = jnp.dot(weights, loc[v, b], preferred_element_type=jnp.float32)
        outbuf[v, :, block_of(b)] = increment.astype(jnp.bfloat16)
        there = pl.ds(pl.multiple_of(place * width + b * size, size), size)

        def give(k, _):
            peer = lax.rem(seat + k, places)
            theirs = pl.ds(pl.multiple_of(peer * rows, rows), rows)
            pltpu.make_async_remote_copy(
                src_ref=outbuf.at[v, theirs, block_of(b)],
                dst_ref=out.at[v, :, there],
                send_sem=out_send,
                recv_sem=out_recv,
                device_id=(half * places + peer, part),
                device_id_type=MESH,
            ).start()
            return 0

        lax.fori_loop(1, places, give, 0)
        pltpu.make_async_copy(outbuf.at[v, seat_rows, block_of(b)], out.at[v, :, there], keep_sem).start()

    def answers(v):
        def step(b, _):
            answer(v, b)
            return 0

        lax.fori_loop(0, per, step, 0)

    at_landed()

    @pl.when(leads)
    def _():
        localize(0)
        for v in range(1, variables):
            arrived(v)
            center_all(v)
            localize(v)

    w_landed()

    @pl.when(leads)
    def _():
        for v in range(variables):
            answers(v)

    @pl.when(jnp.logical_not(leads))
    def _():
        for v in range(variables):
            def step(b, _, v=v):
                loc_copy(v, b).wait_recv()
                answer(v, b)
                return 0

            lax.fori_loop(0, per, step, 0)

    @pl.when(leads)
    def _():
        for v in range(variables):
            def sent(b, _, v=v):
                loc_copy(v, b).wait_send()
                return 0

            lax.fori_loop(0, per, sent, 0)

    for v in range(variables):
        @pl.when(leads)
        def _():
            block = rin.at[v, pl.ds(0, (places - 1) * rows)]
            pltpu.make_async_copy(block, block, in_send.at[v]).wait()

        @pl.when(jnp.logical_not(leads))
        def _():
            block = rin.at[v, pl.ds(0, places * rows)]
            pltpu.make_async_copy(block, block, in_send.at[v]).wait()

    @pl.when(is_guest)
    def _():
        block = guest_in.at[pl.ds(0, rows)]
        pltpu.make_async_copy(block, block, guest_send).wait()

    @pl.when(jnp.logical_not(is_guest))
    def _():
        block = guest_in.at[pl.ds(0, 2 * rows)]
        pltpu.make_async_copy(block, block, guest_send).wait()

    for side in range(2):
        @pl.when(device_of(side, keeper) != me)
        def _():
            for i in range(len(small)):
                small_remote(i, side).wait_send()

    pltpu.make_async_copy(others, others, values_send).wait()
    pltpu.make_async_copy(others_rows, others_rows, inn_send).wait()
    kept = outbuf.at[:, pl.ds(0, rows), :]
    pltpu.make_async_copy(kept, kept, keep_sem).wait()
    block = outbuf.at[:, pl.ds(0, (places - 1) * rows), :]
    pltpu.make_async_copy(block, block, out_send).wait()
    pltpu.make_async_copy(block, block, out_recv).wait()


def finish(state, increment):
    parts = 6
    depth, rows, cells = state.shape
    width = cells * depth // parts

    def body(given, added, out, left, right, held, came, went):
        def piece(i):
            per = parts // depth
            return i // per, slice(None), pl.ds((i % per) * width, width)

        reads = [pltpu.make_async_copy(given.at[piece(i)], left.at[piece(i)], came.at[0, i]) for i in range(parts)]
        more = [pltpu.make_async_copy(added.at[piece(i)], right.at[piece(i)], came.at[1, i]) for i in range(parts)]
        writes = [pltpu.make_async_copy(held.at[piece(i)], out.at[piece(i)], went.at[i]) for i in range(parts)]
        for i in range(parts):
            reads[i].start()
            more[i].start()
        for i in range(parts):
            reads[i].wait()
            more[i].wait()
            held[piece(i)] = (
                left[piece(i)].astype(jnp.float32) + right[piece(i)].astype(jnp.float32)
            ).astype(jnp.bfloat16)
            writes[i].start()
        for copy in writes:
            copy.wait()

    anywhere = pl.BlockSpec(memory_space=pl.ANY)
    return pl.pallas_call(
        body,
        out_shape=jax.ShapeDtypeStruct(state.shape, state.dtype),
        in_specs=[anywhere, anywhere],
        out_specs=anywhere,
        scratch_shapes=[
            pltpu.VMEM(state.shape, state.dtype),
            pltpu.VMEM(state.shape, state.dtype),
            pltpu.VMEM(state.shape, state.dtype),
            pltpu.SemaphoreType.DMA((2, parts)),
            pltpu.SemaphoreType.DMA((parts,)),
        ],
    )(state, increment)


def on_device(n, state, obs_noise, obs_values, obs_weights, tapers, pair_source, pair_taper):
    variables, rows, cells = state.shape
    members = rows * n
    places = n // 2
    width = cells // places
    blocks, size = obs_weights.shape[1], obs_weights.shape[2]
    per = width // size
    pairs = pair_source.shape[2]
    window = per + 2 * RADIUS
    anywhere = pl.BlockSpec(memory_space=pl.ANY)
    increment = pl.pallas_call(
        functools.partial(kernel, n),
        out_shape=jax.ShapeDtypeStruct(state.shape, state.dtype),
        in_specs=[anywhere] * 7,
        out_specs=anywhere,
        scratch_shapes=[
            pltpu.VMEM((rows, cells), jnp.bfloat16),
            pltpu.VMEM((rows, cells), jnp.bfloat16),
            pltpu.VMEM((rows, cells), jnp.bfloat16),
            pltpu.VMEM((1, cells), jnp.float32),
            pltpu.VMEM((variables, members, width), jnp.bfloat16),
            pltpu.VMEM((members, RADIUS * size), jnp.bfloat16),
            pltpu.VMEM((places * rows, width), jnp.bfloat16),
            pltpu.VMEM((variables, members, width), jnp.bfloat16),
            pltpu.VMEM((window, size, members), jnp.bfloat16),
            pltpu.VMEM((window, places * rows, size), jnp.bfloat16),
            pltpu.VMEM((variables, per, pairs * size, size), jnp.bfloat16),
            pltpu.VMEM(tapers.shape, jnp.float32),
            pltpu.VMEM(tapers.shape, jnp.float32),
            pltpu.VMEM((variables, places * rows, width), jnp.bfloat16),
            pltpu.VMEM((2, blocks, size, size), jnp.bfloat16),
            pltpu.SMEM((2, blocks, pairs), jnp.int32),
            pltpu.SMEM((2, blocks, pairs), jnp.int32),
            pltpu.SemaphoreType.DMA((variables + 5,)),
            pltpu.SemaphoreType.DMA,
            pltpu.SemaphoreType.DMA,
            pltpu.SemaphoreType.DMA((variables,)),
            pltpu.SemaphoreType.DMA((variables,)),
            pltpu.SemaphoreType.DMA,
            pltpu.SemaphoreType.DMA,
            pltpu.SemaphoreType.DMA,
            pltpu.SemaphoreType.DMA,
            pltpu.SemaphoreType.DMA,
            pltpu.SemaphoreType.DMA((3, 2)),
            pltpu.SemaphoreType.DMA((3, 2)),
            pltpu.SemaphoreType.DMA((2, 2)),
            pltpu.SemaphoreType.DMA((2, 2)),
            pltpu.SemaphoreType.DMA((variables, per)),
            pltpu.SemaphoreType.DMA((variables, per)),
            pltpu.SemaphoreType.DMA,
            pltpu.SemaphoreType.DMA,
            pltpu.SemaphoreType.DMA,
        ],
        compiler_params=pltpu.CompilerParams(collective_id=0, has_side_effects=True),
    )(state, obs_noise, obs_values, obs_weights, tapers, pair_source, pair_taper)
    return finish(state, increment)


def solution(mesh):
    placed = (
        P(None, "mem", "patch"),
        P("mem", "patch"),
        P("patch", "mem"),
        P("patch", "mem", None, None),
        P(),
        P("patch", "mem", None),
        P("patch", "mem", None),
    )
    return jax.shard_map(
        functools.partial(on_device, mesh.shape["mem"]),
        mesh=mesh,
        in_specs=placed,
        out_specs=P(None, "mem", "patch"),
        check_vma=False,
    )
```

```python
import functools

import jax
import jax.numpy as jnp
from jax import lax
from jax.experimental import pallas as pl
from jax.experimental.pallas import tpu as pltpu
from jax.sharding import PartitionSpec as P

RADIUS = 2
MESH = pl.DeviceIdType.MESH


def seat_of(place, part, places):
    span = places // 4
    leg, step = place // span, place % span
    level = (leg + 1) // 2 % 2
    step = step + (leg % 2) * (span - 1 - 2 * step)
    spot = leg // 2 * span + step
    spot = spot + (part % 2) * (2 * span - 1 - 2 * spot)
    return level * 2 * span + spot


def place_of(seat, part, places):
    span = places // 4
    level, spot = seat // (2 * span), seat % (2 * span)
    spot = spot + (part % 2) * (2 * span - 1 - 2 * spot)
    side, step = spot // span, spot % span
    leg = level + side * (3 - 2 * level)
    step = step + (leg % 2) * (span - 1 - 2 * step)
    return leg * span + step


def kernel(
    n,
    state, noise, obs_values, obs_weights, tapers, pair_source, pair_taper,
    out,
    own_state, own_noise, innov, values, rin, guest_in, inn, anom, win_at, win_w, loc, taper_in, taper_t, outbuf,
    weights_in, source_in, choice_in,
    local_sem, values_send, values_recv, in_send, in_recv, guest_send, guest_recv, guest_local,
    inn_send, inn_recv, small_send, small_recv, halo_send, halo_recv, loc_send, loc_recv,
    out_send, out_recv, keep_sem,
):
    me = lax.axis_index("mem")
    part = lax.axis_index("patch")
    variables, rows, cells = state.shape
    places = n // 2
    leads_each = places // 2
    width = cells // places
    owned = cells // n
    blocks, size = obs_weights.shape[1], obs_weights.shape[2]
    per = width // size
    pairs = pair_source.shape[2]
    members = n * rows
    half, seat = me // places, me % places
    place = place_of(seat, part, places)
    leads = place // leads_each == half
    low, high = leads_each - 1, leads_each
    is_guest = jnp.logical_and(leads, jnp.logical_or(place == low, place == high))
    edge = RADIUS * size

    def device_of(side, where):
        return side * places + seat_of(where, part, places)

    def lead_of(where):
        return device_of(where // leads_each, where)

    def columns(where):
        return pl.ds(pl.multiple_of(where * width, width), width)

    barrier = pltpu.get_barrier_semaphore()

    def greet(k, _):
        peer = lax.rem(me + k, n)
        pl.semaphore_signal(barrier, inc=1, device_id=(peer, part), device_id_type=MESH)
        return 0

    lax.fori_loop(1, n, greet, 0)

    my_rows = pl.ds(pl.multiple_of(me * rows, rows), rows)
    seat_rows = pl.ds(pl.multiple_of(seat * rows, rows), rows)
    mine = columns(place)

    own_copies = [
        pltpu.make_async_copy(state.at[0], own_state, local_sem.at[variables]),
        pltpu.make_async_copy(noise, own_noise, local_sem.at[variables + 1]),
    ]
    for copy in own_copies:
        copy.start()
    taper_copy = pltpu.make_async_copy(tapers, taper_in, local_sem.at[variables + 2])
    taper_copy.start()
    my_values = values.at[:, pl.ds(pl.multiple_of(me * owned, owned), owned)]
    values_copy = pltpu.make_async_copy(obs_values, my_values, local_sem.at[variables + 3])
    values_copy.start()

    raw_local = [
        pltpu.make_async_copy(state.at[v, :, mine], rin.at[v, my_rows], local_sem.at[v]) for v in range(variables)
    ]

    @pl.when(leads)
    def _():
        for copy in raw_local:
            copy.start()

    pl.semaphore_wait(barrier, n - 1)

    def send_values(k, _):
        pltpu.make_async_remote_copy(
            src_ref=obs_values,
            dst_ref=my_values,
            send_sem=values_send,
            recv_sem=values_recv,
            device_id=(lax.rem(me + k, n), part),
            device_id_type=MESH,
        ).start()
        return 0

    lax.fori_loop(1, n, send_values, 0)

    def send_raw(v, side):
        def send(k, _):
            where = side * leads_each + lax.rem(seat + k, leads_each)
            peer = lead_of(where)

            @pl.when(peer != me)
            def _():
                pltpu.make_async_remote_copy(
                    src_ref=state.at[v, :, columns(where)],
                    dst_ref=rin.at[v, my_rows],
                    send_sem=in_send.at[v],
                    recv_sem=in_recv.at[v],
                    device_id=(peer, part),
                    device_id_type=MESH,
                ).start()

            return 0

        lax.fori_loop(0, leads_each, send, 0)

    def edge_of(host):
        start = high * width if host == low else high * width - edge
        return state.at[0, :, pl.ds(start, edge)]

    def send_guests():
        for host in (low, high):
            peer = lead_of(host)

            @pl.when(peer != me)
            def _():
                pltpu.make_async_remote_copy(
                    src_ref=edge_of(host),
                    dst_ref=guest_in.at[my_rows],
                    send_sem=guest_send,
                    recv_sem=guest_recv,
                    device_id=(peer, part),
                    device_id_type=MESH,
                ).start()

            @pl.when(peer == me)
            def _():
                pltpu.make_async_copy(edge_of(host), guest_in.at[my_rows], guest_local).start()

    send_raw(0, 1 - half)
    send_guests()
    send_raw(0, half)

    slot = me % 2
    keeper = me // 2
    small = [
        (obs_weights.at[0], weights_in),
        (pair_source.at[0], source_in),
        (pair_taper.at[0], choice_in),
    ]

    def small_remote(i, side):
        return pltpu.make_async_remote_copy(
            src_ref=small[i][0],
            dst_ref=small[i][1].at[slot],
            send_sem=small_send.at[i, side],
            recv_sem=small_recv.at[i, slot],
            device_id=(device_of(side, keeper), part),
            device_id_type=MESH,
        )

    for side in range(2):
        @pl.when(device_of(side, keeper) != me)
        def _():
            for i in range(len(small)):
                small_remote(i, side).start()

        @pl.when(device_of(side, keeper) == me)
        def _():
            for i in range(len(small)):
                pltpu.make_async_copy(small[i][0], small[i][1].at[slot], small_recv.at[i, slot]).start()

    def small_arrived():
        for i in range(len(small)):
            for s in range(2):
                here = small[i][1].at[s]
                pltpu.make_async_copy(here, here, small_recv.at[i, s]).wait()

    for copy in own_copies:
        copy.wait()
    values_copy.wait()
    others = values.at[:, pl.ds(0, (n - 1) * owned)]
    pltpu.make_async_copy(others, others, values_recv).wait()

    def innovate(p, _):
        here = columns(p)
        innov[:, here] = (
            values[:, here] + own_noise[:, here].astype(jnp.float32) - own_state[:, here].astype(jnp.float32)
        ).astype(jnp.bfloat16)
        return 0

    lax.fori_loop(0, places, innovate, 0)

    def send_innov(k, _):
        where = lax.rem(place + k, places)
        pltpu.make_async_remote_copy(
            src_ref=innov.at[:, columns(where)],
            dst_ref=inn.at[seat_rows],
            send_sem=inn_send,
            recv_sem=inn_recv,
            device_id=(device_of(half, where), part),
            device_id_type=MESH,
        ).start()
        return 0

    lax.fori_loop(1, places, send_innov, 0)
    inn_copy = pltpu.make_async_copy(innov.at[:, mine], inn.at[seat_rows], local_sem.at[variables + 4])
    inn_copy.start()

    def send_rest():
        for v in range(1, variables):
            send_raw(v, 1 - half)
            send_raw(v, half)

    @pl.when(jnp.logical_not(leads))
    def _():
        send_rest()


    taper_copy.wait()

    def flip(k, _):
        taper_t[k] = taper_in[k].T * (1.0 / (members - 1))
        return 0

    lax.fori_loop(0, tapers.shape[0], flip, 0)

    remote_rows = pl.ds(0, (n - 1) * rows)

    def arrived(v):
        raw_local[v].wait()
        block = rin.at[v, remote_rows]
        pltpu.make_async_copy(block, block, in_recv.at[v]).wait()

    def centered(array):
        numbers = array.astype(jnp.float32)
        center = jnp.sum(numbers, axis=0, keepdims=True) * (1.0 / members)
        return (numbers - center).astype(jnp.bfloat16)

    def block_of(b):
        return pl.ds(pl.multiple_of(b * size, size), size)

    def exchange(window, index, before, after):
        left = pltpu.make_async_remote_copy(
            src_ref=window.at[pl.ds(RADIUS, RADIUS)],
            dst_ref=window.at[pl.ds(RADIUS + per, RADIUS)],
            send_sem=halo_send.at[index, 0],
            recv_sem=halo_recv.at[index, 0],
            device_id=(device_of(half, jnp.maximum(place - 1, 0)), part),
            device_id_type=MESH,
        )
        right = pltpu.make_async_remote_copy(
            src_ref=window.at[pl.ds(per, RADIUS)],
            dst_ref=window.at[pl.ds(0, RADIUS)],
            send_sem=halo_send.at[index, 1],
            recv_sem=halo_recv.at[index, 1],
            device_id=(device_of(half, jnp.minimum(place + 1, places - 1)), part),
            device_id_type=MESH,
        )

        def start(side):
            @pl.when((before, after)[side])
            def _():
                (left, right)[side].start()

        def landed():
            @pl.when(before)
            def _():
                left.wait_send()
                right.wait_recv()

            @pl.when(after)
            def _():
                right.wait_send()
                left.wait_recv()

        return start, landed

    at_start, at_landed = exchange(
        win_at,
        0,
        jnp.logical_and(leads, jnp.logical_and(place > 0, place != high)),
        jnp.logical_and(leads, jnp.logical_and(place < places - 1, place != low)),
    )
    w_start, w_landed = exchange(win_w, 1, place > 0, place < places - 1)

    @pl.when(leads)
    def _():
        arrived(0)

        def prepare(b, _):
            first = centered(rin[0, :, block_of(b)])
            anom[0, :, block_of(b)] = first
            win_at[RADIUS + b] = first.T
            return 0

        lax.fori_loop(0, RADIUS, prepare, 0)
        at_start(0)
        lax.fori_loop(RADIUS, per, prepare, 0)
        at_start(1)
        send_rest()

    small_arrived()
    inn_copy.wait()
    others_rows = inn.at[pl.ds(0, (places - 1) * rows)]
    pltpu.make_async_copy(others_rows, others_rows, inn_recv).wait()

    def weigh(b, _):
        win_w[RADIUS + b] = lax.dot_general(
            inn[:, block_of(b)],
            weights_in[b // blocks, b % blocks],
            (((1,), (1,)), ((), ())),
            preferred_element_type=jnp.float32,
        ).astype(jnp.bfloat16)
        return 0

    lax.fori_loop(0, per, weigh, 0)
    for side in range(2):
        w_start(side)


    @pl.when(is_guest)
    def _():
        pltpu.make_async_copy(guest_in.at[my_rows], guest_in.at[my_rows], guest_local).wait()
        block = guest_in.at[remote_rows]
        pltpu.make_async_copy(block, block, guest_recv).wait()
        start = jnp.where(place == low, RADIUS + per, 0)
        for b in range(RADIUS):
            win_at[start + b] = centered(guest_in[:, b * size : (b + 1) * size]).T

    base = place * per - RADIUS

    def near(b, j):
        return jnp.clip(source_in[b // blocks, b % blocks, j] - base, 0, win_at.shape[0] - 1)

    def loc_copy(v, b):
        return pltpu.make_async_remote_copy(
            src_ref=loc.at[v, b],
            dst_ref=loc.at[v, b],
            send_sem=loc_send.at[v, b],
            recv_sem=loc_recv.at[v, b],
            device_id=(device_of(1 - half, place), part),
            device_id_type=MESH,
        )

    def localize(v):
        def step(b, _):
            for j in range(pairs):
                covariance = jnp.dot(
                    win_at[near(b, j)],
                    anom[v, :, block_of(b)],
                    preferred_element_type=jnp.float32,
                )
                loc[v, b, pl.ds(j * size, size), :] = (
                    covariance * taper_t[choice_in[b // blocks, b % blocks, j]]
                ).astype(jnp.bfloat16)
            loc_copy(v, b).start()
            return 0

        lax.fori_loop(0, per, step, 0)

    def center_all(v):
        def step(b, _):
            anom[v, :, block_of(b)] = centered(rin[v, :, block_of(b)])
            return 0

        lax.fori_loop(0, per, step, 0)

    def answer(v, b):
        weights = jnp.concatenate([win_w[near(b, j)] for j in range(pairs)], axis=1)
        increment = jnp.dot(weights, loc[v, b], preferred_element_type=jnp.float32)
        outbuf[v, :, block_of(b)] = increment.astype(jnp.bfloat16)
        there = pl.ds(pl.multiple_of(place * width + b * size, size), size)

        def give(k, _):
            peer = lax.rem(seat + k, places)
            theirs = pl.ds(pl.multiple_of(peer * rows, rows), rows)
            pltpu.make_async_remote_copy(
                src_ref=outbuf.at[v, theirs, block_of(b)],
                dst_ref=out.at[v, :, there],
                send_sem=out_send,
                recv_sem=out_recv,
                device_id=(half * places + peer, part),
                device_id_type=MESH,
            ).start()
            return 0

        lax.fori_loop(1, places, give, 0)
        pltpu.make_async_copy(outbuf.at[v, seat_rows, block_of(b)], out.at[v, :, there], keep_sem).start()

    def answers(v):
        def step(b, _):
            answer(v, b)
            return 0

        lax.fori_loop(0, per, step, 0)

    at_landed()

    @pl.when(leads)
    def _():
        localize(0)
        for v in range(1, variables):
            arrived(v)
            center_all(v)
            localize(v)

    w_landed()

    @pl.when(leads)
    def _():
        for v in range(variables):
            answers(v)

    @pl.when(jnp.logical_not(leads))
    def _():
        for v in range(variables):
            def step(b, _, v=v):
                loc_copy(v, b).wait_recv()
                answer(v, b)
                return 0

            lax.fori_loop(0, per, step, 0)

    @pl.when(leads)
    def _():
        for v in range(variables):
            def sent(b, _, v=v):
                loc_copy(v, b).wait_send()
                return 0

            lax.fori_loop(0, per, sent, 0)

    for v in range(variables):
        @pl.when(leads)
        def _():
            block = rin.at[v, pl.ds(0, (places - 1) * rows)]
            pltpu.make_async_copy(block, block, in_send.at[v]).wait()

        @pl.when(jnp.logical_not(leads))
        def _():
            block = rin.at[v, pl.ds(0, places * rows)]
            pltpu.make_async_copy(block, block, in_send.at[v]).wait()

    @pl.when(is_guest)
    def _():
        block = guest_in.at[pl.ds(0, rows)]
        pltpu.make_async_copy(block, block, guest_send).wait()

    @pl.when(jnp.logical_not(is_guest))
    def _():
        block = guest_in.at[pl.ds(0, 2 * rows)]
        pltpu.make_async_copy(block, block, guest_send).wait()

    for side in range(2):
        @pl.when(device_of(side, keeper) != me)
        def _():
            for i in range(len(small)):
                small_remote(i, side).wait_send()

    pltpu.make_async_copy(others, others, values_send).wait()
    pltpu.make_async_copy(others_rows, others_rows, inn_send).wait()
    kept = outbuf.at[:, pl.ds(0, rows), :]
    pltpu.make_async_copy(kept, kept, keep_sem).wait()
    block = outbuf.at[:, pl.ds(0, (places - 1) * rows), :]
    pltpu.make_async_copy(block, block, out_send).wait()
    pltpu.make_async_copy(block, block, out_recv).wait()


def finish(state, increment):
    parts = 6
    depth, rows, cells = state.shape
    width = cells * depth // parts

    def body(given, added, out, held, went):
        def piece(i):
            per = parts // depth
            return i // per, slice(None), pl.ds((i % per) * width, width)

        writes = [pltpu.make_async_copy(held.at[piece(i)], out.at[piece(i)], went.at[i]) for i in range(parts)]
        for i in range(parts):
            held[piece(i)] = (
                given[piece(i)].astype(jnp.float32) + added[piece(i)].astype(jnp.float32)
            ).astype(jnp.bfloat16)
            writes[i].start()
        for copy in writes:
            copy.wait()

    near = pl.BlockSpec(memory_space=pltpu.VMEM)
    return pl.pallas_call(
        body,
        out_shape=jax.ShapeDtypeStruct(state.shape, state.dtype),
        in_specs=[near, near],
        out_specs=pl.BlockSpec(memory_space=pltpu.HBM),
        scratch_shapes=[
            pltpu.VMEM(state.shape, state.dtype),
            pltpu.SemaphoreType.DMA((parts,)),
        ],
        compiler_params=pltpu.CompilerParams(vmem_limit_bytes=8 * 1024 * 1024),
    )(state, increment)


def on_device(n, state, obs_noise, obs_values, obs_weights, tapers, pair_source, pair_taper):
    variables, rows, cells = state.shape
    members = rows * n
    places = n // 2
    width = cells // places
    blocks, size = obs_weights.shape[1], obs_weights.shape[2]
    per = width // size
    pairs = pair_source.shape[2]
    window = per + 2 * RADIUS
    anywhere = pl.BlockSpec(memory_space=pl.ANY)
    increment = pl.pallas_call(
        functools.partial(kernel, n),
        out_shape=jax.ShapeDtypeStruct(state.shape, state.dtype),
        in_specs=[pl.BlockSpec(memory_space=pltpu.HBM)] * 7,
        out_specs=anywhere,
        scratch_shapes=[
            pltpu.VMEM((rows, cells), jnp.bfloat16),
            pltpu.VMEM((rows, cells), jnp.bfloat16),
            pltpu.VMEM((rows, cells), jnp.bfloat16),
            pltpu.VMEM((1, cells), jnp.float32),
            pltpu.VMEM((variables, members, width), jnp.bfloat16),
            pltpu.VMEM((members, RADIUS * size), jnp.bfloat16),
            pltpu.VMEM((places * rows, width), jnp.bfloat16),
            pltpu.VMEM((variables, members, width), jnp.bfloat16),
            pltpu.VMEM((window, size, members), jnp.bfloat16),
            pltpu.VMEM((window, places * rows, size), jnp.bfloat16),
            pltpu.VMEM((variables, per, pairs * size, size), jnp.bfloat16),
            pltpu.VMEM(tapers.shape, jnp.float32),
            pltpu.VMEM(tapers.shape, jnp.float32),
            pltpu.VMEM((variables, places * rows, width), jnp.bfloat16),
            pltpu.VMEM((2, blocks, size, size), jnp.bfloat16),
            pltpu.SMEM((2, blocks, pairs), jnp.int32),
            pltpu.SMEM((2, blocks, pairs), jnp.int32),
            pltpu.SemaphoreType.DMA((variables + 5,)),
            pltpu.SemaphoreType.DMA,
            pltpu.SemaphoreType.DMA,
            pltpu.SemaphoreType.DMA((variables,)),
            pltpu.SemaphoreType.DMA((variables,)),
            pltpu.SemaphoreType.DMA,
            pltpu.SemaphoreType.DMA,
            pltpu.SemaphoreType.DMA,
            pltpu.SemaphoreType.DMA,
            pltpu.SemaphoreType.DMA,
            pltpu.SemaphoreType.DMA((3, 2)),
            pltpu.SemaphoreType.DMA((3, 2)),
            pltpu.SemaphoreType.DMA((2, 2)),
            pltpu.SemaphoreType.DMA((2, 2)),
            pltpu.SemaphoreType.DMA((variables, per)),
            pltpu.SemaphoreType.DMA((variables, per)),
            pltpu.SemaphoreType.DMA,
            pltpu.SemaphoreType.DMA,
            pltpu.SemaphoreType.DMA,
        ],
        compiler_params=pltpu.CompilerParams(
            collective_id=0, has_side_effects=True, vmem_limit_bytes=24 * 1024 * 1024
        ),
    )(*[pltpu.with_memory_space_constraint(x, pltpu.HBM) for x in (state, obs_noise, obs_values, obs_weights, tapers, pair_source, pair_taper)])
    return finish(state, increment)


def solution(mesh):
    placed = (
        P(None, "mem", "patch"),
        P("mem", "patch"),
        P("patch", "mem"),
        P("patch", "mem", None, None),
        P(),
        P("patch", "mem", None),
        P("patch", "mem", None),
    )
    return jax.shard_map(
        functools.partial(on_device, mesh.shape["mem"]),
        mesh=mesh,
        in_specs=placed,
        out_specs=P(None, "mem", "patch"),
        check_vma=False,
    )
```

```python
import functools

import jax
import jax.numpy as jnp
from jax import lax
from jax.experimental import pallas as pl
from jax.experimental.pallas import tpu as pltpu
from jax.sharding import PartitionSpec as P

RADIUS = 2
MESH = pl.DeviceIdType.MESH


def seat_of(place, part, places):
    span = places // 4
    leg, step = place // span, place % span
    level = (leg + 1) // 2 % 2
    step = step + (leg % 2) * (span - 1 - 2 * step)
    spot = leg // 2 * span + step
    spot = spot + (part % 2) * (2 * span - 1 - 2 * spot)
    return level * 2 * span + spot


def place_of(seat, part, places):
    span = places // 4
    level, spot = seat // (2 * span), seat % (2 * span)
    spot = spot + (part % 2) * (2 * span - 1 - 2 * spot)
    side, step = spot // span, spot % span
    leg = level + side * (3 - 2 * level)
    step = step + (leg % 2) * (span - 1 - 2 * step)
    return leg * span + step


def kernel(
    n,
    state, noise, obs_values, obs_weights, tapers, pair_source, pair_taper,
    out,
    own_state, own_noise, innov, values, rin, guest_in, inn, anom, at_left, at_right, win_w, loc, taper_in, taper_t, outbuf,
    weights_in, source_in, choice_in,
    local_sem, values_send, values_recv, in_send, in_recv, guest_send, guest_recv, guest_local,
    inn_send, inn_recv, small_send, small_recv, halo_send, halo_recv, loc_send, loc_recv,
    out_send, out_recv, keep_sem,
):
    me = lax.axis_index("mem")
    part = lax.axis_index("patch")
    variables, rows, cells = state.shape
    places = n // 2
    leads_each = places // 2
    width = cells // places
    owned = cells // n
    blocks, size = obs_weights.shape[1], obs_weights.shape[2]
    per = width // size
    pairs = pair_source.shape[2]
    members = n * rows
    half, seat = me // places, me % places
    place = place_of(seat, part, places)
    leads = place // leads_each == half
    low, high = leads_each - 1, leads_each
    is_guest = jnp.logical_and(leads, jnp.logical_or(place == low, place == high))
    edge = RADIUS * size

    def device_of(side, where):
        return side * places + seat_of(where, part, places)

    def lead_of(where):
        return device_of(where // leads_each, where)

    def columns(where):
        return pl.ds(pl.multiple_of(where * width, width), width)

    barrier = pltpu.get_barrier_semaphore()

    def greet(k, _):
        peer = lax.rem(me + k, n)
        pl.semaphore_signal(barrier, inc=1, device_id=(peer, part), device_id_type=MESH)
        return 0

    lax.fori_loop(1, n, greet, 0)

    my_rows = pl.ds(pl.multiple_of(me * rows, rows), rows)
    seat_rows = pl.ds(pl.multiple_of(seat * rows, rows), rows)
    mine = columns(place)

    own_copies = [
        pltpu.make_async_copy(state.at[0], own_state, local_sem.at[variables]),
        pltpu.make_async_copy(noise, own_noise, local_sem.at[variables + 1]),
    ]
    for copy in own_copies:
        copy.start()
    taper_copy = pltpu.make_async_copy(tapers, taper_in, local_sem.at[variables + 2])
    taper_copy.start()
    my_values = values.at[:, pl.ds(pl.multiple_of(me * owned, owned), owned)]
    values_copy = pltpu.make_async_copy(obs_values, my_values, local_sem.at[variables + 3])
    values_copy.start()

    raw_local = [
        pltpu.make_async_copy(state.at[v, :, mine], rin.at[v, my_rows], local_sem.at[v]) for v in range(variables)
    ]

    @pl.when(leads)
    def _():
        for copy in raw_local:
            copy.start()

    pl.semaphore_wait(barrier, n - 1)

    def send_values(k, _):
        pltpu.make_async_remote_copy(
            src_ref=obs_values,
            dst_ref=my_values,
            send_sem=values_send,
            recv_sem=values_recv,
            device_id=(lax.rem(me + k, n), part),
            device_id_type=MESH,
        ).start()
        return 0

    lax.fori_loop(1, n, send_values, 0)

    def send_raw(v, side):
        def send(k, _):
            where = side * leads_each + lax.rem(seat + seat // leads_each * (leads_each // 2) + k, leads_each)
            peer = lead_of(where)

            @pl.when(peer != me)
            def _():
                pltpu.make_async_remote_copy(
                    src_ref=state.at[v, :, columns(where)],
                    dst_ref=rin.at[v, my_rows],
                    send_sem=in_send.at[v],
                    recv_sem=in_recv.at[v],
                    device_id=(peer, part),
                    device_id_type=MESH,
                ).start()

            return 0

        lax.fori_loop(0, leads_each, send, 0)

    def edge_of(host):
        start = high * width if host == low else high * width - edge
        return state.at[0, :, pl.ds(start, edge)]

    def send_guests():
        for host in (low, high):
            peer = lead_of(host)

            @pl.when(peer != me)
            def _():
                pltpu.make_async_remote_copy(
                    src_ref=edge_of(host),
                    dst_ref=guest_in.at[my_rows],
                    send_sem=guest_send,
                    recv_sem=guest_recv,
                    device_id=(peer, part),
                    device_id_type=MESH,
                ).start()

            @pl.when(peer == me)
            def _():
                pltpu.make_async_copy(edge_of(host), guest_in.at[my_rows], guest_local).start()

    send_raw(0, 1 - half)
    send_guests()
    send_raw(0, half)

    slot = me % 2
    keeper = me // 2
    small = [
        (obs_weights.at[0], weights_in),
        (pair_source.at[0], source_in),
        (pair_taper.at[0], choice_in),
    ]

    def small_remote(i, side):
        return pltpu.make_async_remote_copy(
            src_ref=small[i][0],
            dst_ref=small[i][1].at[slot],
            send_sem=small_send.at[i, side],
            recv_sem=small_recv.at[i, slot],
            device_id=(device_of(side, keeper), part),
            device_id_type=MESH,
        )

    for side in range(2):
        @pl.when(device_of(side, keeper) != me)
        def _():
            for i in range(len(small)):
                small_remote(i, side).start()

        @pl.when(device_of(side, keeper) == me)
        def _():
            for i in range(len(small)):
                pltpu.make_async_copy(small[i][0], small[i][1].at[slot], small_recv.at[i, slot]).start()

    def small_arrived():
        for i in range(len(small)):
            for s in range(2):
                here = small[i][1].at[s]
                pltpu.make_async_copy(here, here, small_recv.at[i, s]).wait()

    for copy in own_copies:
        copy.wait()
    values_copy.wait()
    others = values.at[:, pl.ds(0, (n - 1) * owned)]
    pltpu.make_async_copy(others, others, values_recv).wait()

    def innovate(p, _):
        here = columns(p)
        innov[:, here] = (
            values[:, here] + own_noise[:, here].astype(jnp.float32) - own_state[:, here].astype(jnp.float32)
        ).astype(jnp.bfloat16)
        return 0

    lax.fori_loop(0, places, innovate, 0)

    def send_innov(k, _):
        where = lax.rem(place + places - k, places)
        pltpu.make_async_remote_copy(
            src_ref=innov.at[:, columns(where)],
            dst_ref=inn.at[seat_rows],
            send_sem=inn_send,
            recv_sem=inn_recv,
            device_id=(device_of(half, where), part),
            device_id_type=MESH,
        ).start()
        return 0

    lax.fori_loop(1, places, send_innov, 0)
    inn_copy = pltpu.make_async_copy(innov.at[:, mine], inn.at[seat_rows], local_sem.at[variables + 4])
    inn_copy.start()

    def send_rest():
        for v in range(1, variables):
            send_raw(v, 1 - half)
            send_raw(v, half)

    @pl.when(jnp.logical_not(leads))
    def _():
        send_rest()


    taper_copy.wait()

    def flip(k, _):
        taper_t[k] = taper_in[k].T * (1.0 / (members - 1))
        return 0

    lax.fori_loop(0, tapers.shape[0], flip, 0)

    remote_rows = pl.ds(0, (n - 1) * rows)

    def arrived(v):
        raw_local[v].wait()
        block = rin.at[v, remote_rows]
        pltpu.make_async_copy(block, block, in_recv.at[v]).wait()

    def centered(array):
        numbers = array.astype(jnp.float32)
        center = jnp.sum(numbers, axis=0, keepdims=True) * (1.0 / members)
        return (numbers - center).astype(jnp.bfloat16)

    def block_of(b):
        return pl.ds(pl.multiple_of(b * size, size), size)

    def exchange(index, before, after, sources, targets):
        left = pltpu.make_async_remote_copy(
            src_ref=sources[0],
            dst_ref=targets[1],
            send_sem=halo_send.at[index, 0],
            recv_sem=halo_recv.at[index, 0],
            device_id=(device_of(half, jnp.maximum(place - 1, 0)), part),
            device_id_type=MESH,
        )
        right = pltpu.make_async_remote_copy(
            src_ref=sources[1],
            dst_ref=targets[0],
            send_sem=halo_send.at[index, 1],
            recv_sem=halo_recv.at[index, 1],
            device_id=(device_of(half, jnp.minimum(place + 1, places - 1)), part),
            device_id_type=MESH,
        )

        def start(side):
            @pl.when((before, after)[side])
            def _():
                (left, right)[side].start()

        def landed(side):
            @pl.when((before, after)[side])
            def _():
                (left, right)[side].wait_send()
                (right, left)[side].wait_recv()

        return start, landed

    at_start, at_landed = exchange(
        0,
        jnp.logical_and(leads, jnp.logical_and(place > 0, place != high)),
        jnp.logical_and(leads, jnp.logical_and(place < places - 1, place != low)),
        (at_left.at[pl.ds(RADIUS, RADIUS)], at_right.at[pl.ds(per - RADIUS, RADIUS)]),
        (at_left.at[pl.ds(0, RADIUS)], at_right.at[pl.ds(per, RADIUS)]),
    )
    w_start, w_landed = exchange(
        1,
        place > 0,
        place < places - 1,
        (win_w.at[pl.ds(RADIUS, RADIUS)], win_w.at[pl.ds(per, RADIUS)]),
        (win_w.at[pl.ds(0, RADIUS)], win_w.at[pl.ds(RADIUS + per, RADIUS)]),
    )

    @pl.when(leads)
    def _():
        arrived(0)

        def prepare(b, _):
            first = centered(rin[0, :, block_of(b)])
            anom[0, :, block_of(b)] = first
            flipped = first.T
            at_left[RADIUS + b] = flipped
            at_right[b] = flipped
            return 0

        lax.fori_loop(0, RADIUS, prepare, 0)
        at_start(0)
        lax.fori_loop(RADIUS, per, prepare, 0)
        at_start(1)
        send_rest()

    small_arrived()
    inn_copy.wait()
    others_rows = inn.at[pl.ds(0, (places - 1) * rows)]
    pltpu.make_async_copy(others_rows, others_rows, inn_recv).wait()

    def weigh(b, _):
        win_w[RADIUS + b] = lax.dot_general(
            inn[:, block_of(b)],
            weights_in[b // blocks, b % blocks],
            (((1,), (1,)), ((), ())),
            preferred_element_type=jnp.float32,
        ).astype(jnp.bfloat16)
        return 0

    lax.fori_loop(0, per, weigh, 0)
    for side in range(2):
        w_start(side)


    @pl.when(is_guest)
    def _():
        pltpu.make_async_copy(guest_in.at[my_rows], guest_in.at[my_rows], guest_local).wait()
        block = guest_in.at[remote_rows]
        pltpu.make_async_copy(block, block, guest_recv).wait()
        for b in range(RADIUS):
            flipped = centered(guest_in[:, b * size : (b + 1) * size]).T

            @pl.when(place == low)
            def _():
                at_right[per + b] = flipped

            @pl.when(place == high)
            def _():
                at_left[b] = flipped

    base = place * per - RADIUS

    def near(b, j):
        return jnp.clip(source_in[b // blocks, b % blocks, j] - base, 0, win_w.shape[0] - 1)

    turned = place // (places // 4) % 2
    bound = per // 2

    def source_block(side, b, j):
        if side:
            return at_right[jnp.clip(near(b, j) - RADIUS, 0, at_right.shape[0] - 1)]
        return at_left[jnp.minimum(near(b, j), at_left.shape[0] - 1)]

    def loc_copy(v, b):
        return pltpu.make_async_remote_copy(
            src_ref=loc.at[v, b],
            dst_ref=loc.at[v, b],
            send_sem=loc_send.at[v, b],
            recv_sem=loc_recv.at[v, b],
            device_id=(device_of(1 - half, place), part),
            device_id_type=MESH,
        )

    def localize(v, side):
        def step(b, _):
            for j in range(pairs):
                covariance = jnp.dot(
                    source_block(side, b, j),
                    anom[v, :, block_of(b)],
                    preferred_element_type=jnp.float32,
                )
                loc[v, b, pl.ds(j * size, size), :] = (
                    covariance * taper_t[choice_in[b // blocks, b % blocks, j]]
                ).astype(jnp.bfloat16)
            loc_copy(v, b).start()
            return 0

        lax.fori_loop(side * bound, side * bound + bound, step, 0)

    def center_all(v):
        def step(b, _):
            anom[v, :, block_of(b)] = centered(rin[v, :, block_of(b)])
            return 0

        lax.fori_loop(0, per, step, 0)

    def answer(v, b):
        weights = jnp.concatenate([win_w[near(b, j)] for j in range(pairs)], axis=1)
        increment = jnp.dot(weights, loc[v, b], preferred_element_type=jnp.float32)
        outbuf[v, :, block_of(b)] = increment.astype(jnp.bfloat16)
        there = pl.ds(pl.multiple_of(place * width + b * size, size), size)

        def give(k, _):
            peer = lax.rem(seat + k, places)
            theirs = pl.ds(pl.multiple_of(peer * rows, rows), rows)
            pltpu.make_async_remote_copy(
                src_ref=outbuf.at[v, theirs, block_of(b)],
                dst_ref=out.at[v, :, there],
                send_sem=out_send,
                recv_sem=out_recv,
                device_id=(half * places + peer, part),
                device_id_type=MESH,
            ).start()
            return 0

        lax.fori_loop(1, places, give, 0)
        pltpu.make_async_copy(outbuf.at[v, seat_rows, block_of(b)], out.at[v, :, there], keep_sem).start()

    def answers(v):
        def step(b, _):
            answer(v, b)
            return 0

        lax.fori_loop(0, per, step, 0)

    early = max(variables - 1, 1)

    @pl.when(leads)
    def _():
        def stage(k, _):
            for side in range(2):
                @pl.when((k + turned) % 2 == side)
                def _():
                    at_landed(side)
                    localize(0, side)

                    @pl.when(k == 0)
                    def _():
                        for v in range(1, early):
                            arrived(v)
                            center_all(v)

                    for v in range(1, early):
                        localize(v, side)

            return 0

        lax.fori_loop(0, 2, stage, 0)
        for v in range(early, variables):
            arrived(v)
            center_all(v)
            for side in range(2):
                localize(v, side)

    w_landed(0)
    w_landed(1)

    @pl.when(leads)
    def _():
        for v in range(variables):
            answers(v)

    @pl.when(jnp.logical_not(leads))
    def _():
        for v in range(variables):
            block = rin.at[v, pl.ds(0, places * rows)]
            pltpu.make_async_copy(block, block, in_send.at[v]).wait()

    @pl.when(jnp.logical_not(leads))
    def _():
        def reply(v, b):
            loc_copy(v, b).wait_recv()
            answer(v, b)

        def stage(k, _):
            for v in range(early):
                def step(i, _, v=v):
                    reply(v, (k + turned) % 2 * bound + i)
                    return 0

                lax.fori_loop(0, bound, step, 0)
            return 0

        lax.fori_loop(0, 2, stage, 0)
        for v in range(early, variables):
            def step(b, _, v=v):
                reply(v, b)
                return 0

            lax.fori_loop(0, per, step, 0)

    @pl.when(leads)
    def _():
        for v in range(variables):
            def sent(b, _, v=v):
                loc_copy(v, b).wait_send()
                return 0

            lax.fori_loop(0, per, sent, 0)

    for v in range(variables):
        @pl.when(leads)
        def _():
            block = rin.at[v, pl.ds(0, (places - 1) * rows)]
            pltpu.make_async_copy(block, block, in_send.at[v]).wait()


    @pl.when(is_guest)
    def _():
        block = guest_in.at[pl.ds(0, rows)]
        pltpu.make_async_copy(block, block, guest_send).wait()

    @pl.when(jnp.logical_not(is_guest))
    def _():
        block = guest_in.at[pl.ds(0, 2 * rows)]
        pltpu.make_async_copy(block, block, guest_send).wait()

    for side in range(2):
        @pl.when(device_of(side, keeper) != me)
        def _():
            for i in range(len(small)):
                small_remote(i, side).wait_send()

    pltpu.make_async_copy(others, others, values_send).wait()
    pltpu.make_async_copy(others_rows, others_rows, inn_send).wait()
    kept = outbuf.at[:, pl.ds(0, rows), :]
    pltpu.make_async_copy(kept, kept, keep_sem).wait()
    block = outbuf.at[:, pl.ds(0, (places - 1) * rows), :]
    pltpu.make_async_copy(block, block, out_send).wait()
    pltpu.make_async_copy(block, block, out_recv).wait()


def finish(state, increment):
    parts = 6
    depth, rows, cells = state.shape
    width = cells * depth // parts

    def body(given, added, out, held, went):
        def piece(i):
            per = parts // depth
            return i // per, slice(None), pl.ds((i % per) * width, width)

        writes = [pltpu.make_async_copy(held.at[piece(i)], out.at[piece(i)], went.at[i]) for i in range(parts)]
        for i in range(parts):
            held[piece(i)] = (
                given[piece(i)].astype(jnp.float32) + added[piece(i)].astype(jnp.float32)
            ).astype(jnp.bfloat16)
            writes[i].start()
        for copy in writes:
            copy.wait()

    near = pl.BlockSpec(memory_space=pltpu.VMEM)
    return pl.pallas_call(
        body,
        out_shape=jax.ShapeDtypeStruct(state.shape, state.dtype),
        in_specs=[near, near],
        out_specs=pl.BlockSpec(memory_space=pltpu.HBM),
        scratch_shapes=[
            pltpu.VMEM(state.shape, state.dtype),
            pltpu.SemaphoreType.DMA((parts,)),
        ],
        compiler_params=pltpu.CompilerParams(vmem_limit_bytes=8 * 1024 * 1024),
    )(state, increment)


def on_device(n, state, obs_noise, obs_values, obs_weights, tapers, pair_source, pair_taper):
    variables, rows, cells = state.shape
    members = rows * n
    places = n // 2
    width = cells // places
    blocks, size = obs_weights.shape[1], obs_weights.shape[2]
    per = width // size
    pairs = pair_source.shape[2]
    window = per + 2 * RADIUS
    anywhere = pl.BlockSpec(memory_space=pl.ANY)
    increment = pl.pallas_call(
        functools.partial(kernel, n),
        out_shape=jax.ShapeDtypeStruct(state.shape, state.dtype),
        in_specs=[pl.BlockSpec(memory_space=pltpu.HBM)] * 7,
        out_specs=anywhere,
        scratch_shapes=[
            pltpu.VMEM((rows, cells), jnp.bfloat16),
            pltpu.VMEM((rows, cells), jnp.bfloat16),
            pltpu.VMEM((rows, cells), jnp.bfloat16),
            pltpu.VMEM((1, cells), jnp.float32),
            pltpu.VMEM((variables, members, width), jnp.bfloat16),
            pltpu.VMEM((members, RADIUS * size), jnp.bfloat16),
            pltpu.VMEM((places * rows, width), jnp.bfloat16),
            pltpu.VMEM((variables, members, width), jnp.bfloat16),
            pltpu.VMEM((per + RADIUS, size, members), jnp.bfloat16),
            pltpu.VMEM((per + RADIUS, size, members), jnp.bfloat16),
            pltpu.VMEM((window, places * rows, size), jnp.bfloat16),
            pltpu.VMEM((variables, per, pairs * size, size), jnp.bfloat16),
            pltpu.VMEM(tapers.shape, jnp.float32),
            pltpu.VMEM(tapers.shape, jnp.float32),
            pltpu.VMEM((variables, places * rows, width), jnp.bfloat16),
            pltpu.VMEM((2, blocks, size, size), jnp.bfloat16),
            pltpu.SMEM((2, blocks, pairs), jnp.int32),
            pltpu.SMEM((2, blocks, pairs), jnp.int32),
            pltpu.SemaphoreType.DMA((variables + 5,)),
            pltpu.SemaphoreType.DMA,
            pltpu.SemaphoreType.DMA,
            pltpu.SemaphoreType.DMA((variables,)),
            pltpu.SemaphoreType.DMA((variables,)),
            pltpu.SemaphoreType.DMA,
            pltpu.SemaphoreType.DMA,
            pltpu.SemaphoreType.DMA,
            pltpu.SemaphoreType.DMA,
            pltpu.SemaphoreType.DMA,
            pltpu.SemaphoreType.DMA((3, 2)),
            pltpu.SemaphoreType.DMA((3, 2)),
            pltpu.SemaphoreType.DMA((2, 2)),
            pltpu.SemaphoreType.DMA((2, 2)),
            pltpu.SemaphoreType.DMA((variables, per)),
            pltpu.SemaphoreType.DMA((variables, per)),
            pltpu.SemaphoreType.DMA,
            pltpu.SemaphoreType.DMA,
            pltpu.SemaphoreType.DMA,
        ],
        compiler_params=pltpu.CompilerParams(
            collective_id=0, has_side_effects=True, vmem_limit_bytes=24 * 1024 * 1024
        ),
    )(*[pltpu.with_memory_space_constraint(x, pltpu.HBM) for x in (state, obs_noise, obs_values, obs_weights, tapers, pair_source, pair_taper)])
    return finish(state, increment)


def solution(mesh):
    placed = (
        P(None, "mem", "patch"),
        P("mem", "patch"),
        P("patch", "mem"),
        P("patch", "mem", None, None),
        P(),
        P("patch", "mem", None),
        P("patch", "mem", None),
    )
    return jax.shard_map(
        functools.partial(on_device, mesh.shape["mem"]),
        mesh=mesh,
        in_specs=placed,
        out_specs=P(None, "mem", "patch"),
        check_vma=False,
    )
```

```python
import functools

import jax
import jax.numpy as jnp
from jax import lax
from jax.experimental import pallas as pl
from jax.experimental.pallas import tpu as pltpu
from jax.sharding import PartitionSpec as P

RADIUS = 2
MESH = pl.DeviceIdType.MESH


def seat_of(place, part, places):
    span = places // 4
    leg, step = place // span, place % span
    level = (leg + 1) // 2 % 2
    step = step + (leg % 2) * (span - 1 - 2 * step)
    spot = leg // 2 * span + step
    spot = spot + (part % 2) * (2 * span - 1 - 2 * spot)
    return level * 2 * span + spot


def place_of(seat, part, places):
    span = places // 4
    level, spot = seat // (2 * span), seat % (2 * span)
    spot = spot + (part % 2) * (2 * span - 1 - 2 * spot)
    side, step = spot // span, spot % span
    leg = level + side * (3 - 2 * level)
    step = step + (leg % 2) * (span - 1 - 2 * step)
    return leg * span + step


def kernel(
    n,
    state, noise, obs_values, obs_weights, tapers, pair_source, pair_taper,
    out,
    own_state, own_noise, innov, values, rin, guest_in, inn, anom, at_left, at_right, win_w, loc, taper_in, taper_t, outbuf,
    weights_in, source_in, choice_in,
    local_sem, values_send, values_recv, in_send, in_recv, guest_send, guest_recv, guest_local,
    inn_send, inn_recv, small_send, small_recv, halo_send, halo_recv, loc_send, loc_recv,
    out_send, out_recv, keep_sem,
):
    me = lax.axis_index("mem")
    part = lax.axis_index("patch")
    variables, rows, cells = state.shape
    places = n // 2
    leads_each = places // 2
    width = cells // places
    owned = cells // n
    blocks, size = obs_weights.shape[1], obs_weights.shape[2]
    per = width // size
    pairs = pair_source.shape[2]
    members = n * rows
    half, seat = me // places, me % places
    place = place_of(seat, part, places)
    leads = place // leads_each == half
    low, high = leads_each - 1, leads_each
    is_guest = jnp.logical_and(leads, jnp.logical_or(place == low, place == high))
    edge = RADIUS * size

    def device_of(side, where):
        return side * places + seat_of(where, part, places)

    def lead_of(where):
        return device_of(where // leads_each, where)

    def columns(where):
        return pl.ds(pl.multiple_of(where * width, width), width)

    barrier = pltpu.get_barrier_semaphore()

    def greet(k, _):
        peer = lax.rem(me + k, n)
        pl.semaphore_signal(barrier, inc=1, device_id=(peer, part), device_id_type=MESH)
        return 0

    lax.fori_loop(1, n, greet, 0)

    my_rows = pl.ds(pl.multiple_of(me * rows, rows), rows)
    seat_rows = pl.ds(pl.multiple_of(seat * rows, rows), rows)
    mine = columns(place)

    own_copies = [
        pltpu.make_async_copy(state.at[0], own_state, local_sem.at[variables]),
        pltpu.make_async_copy(noise, own_noise, local_sem.at[variables + 1]),
    ]
    for copy in own_copies:
        copy.start()
    taper_copy = pltpu.make_async_copy(tapers, taper_in, local_sem.at[variables + 2])
    taper_copy.start()
    my_values = values.at[:, pl.ds(pl.multiple_of(me * owned, owned), owned)]
    values_copy = pltpu.make_async_copy(obs_values, my_values, local_sem.at[variables + 3])
    values_copy.start()

    raw_local = [
        pltpu.make_async_copy(state.at[v, :, mine], rin.at[v, my_rows], local_sem.at[v]) for v in range(variables)
    ]

    @pl.when(leads)
    def _():
        for copy in raw_local:
            copy.start()

    pl.semaphore_wait(barrier, n - 1)

    def send_values(k, _):
        pltpu.make_async_remote_copy(
            src_ref=obs_values,
            dst_ref=my_values,
            send_sem=values_send,
            recv_sem=values_recv,
            device_id=(lax.rem(me + k, n), part),
            device_id_type=MESH,
        ).start()
        return 0

    lax.fori_loop(1, n, send_values, 0)

    def send_raw(v, side):
        def send(k, _):
            where = side * leads_each + lax.rem(seat + seat // leads_each * (leads_each // 2) + k, leads_each)
            peer = lead_of(where)

            @pl.when(peer != me)
            def _():
                pltpu.make_async_remote_copy(
                    src_ref=state.at[v, :, columns(where)],
                    dst_ref=rin.at[v, my_rows],
                    send_sem=in_send.at[v],
                    recv_sem=in_recv.at[v],
                    device_id=(peer, part),
                    device_id_type=MESH,
                ).start()

            return 0

        lax.fori_loop(0, leads_each, send, 0)

    def edge_of(host):
        start = high * width if host == low else high * width - edge
        return state.at[0, :, pl.ds(start, edge)]

    def send_guests():
        for host in (low, high):
            peer = lead_of(host)

            @pl.when(peer != me)
            def _():
                pltpu.make_async_remote_copy(
                    src_ref=edge_of(host),
                    dst_ref=guest_in.at[my_rows],
                    send_sem=guest_send,
                    recv_sem=guest_recv,
                    device_id=(peer, part),
                    device_id_type=MESH,
                ).start()

            @pl.when(peer == me)
            def _():
                pltpu.make_async_copy(edge_of(host), guest_in.at[my_rows], guest_local).start()

    send_raw(0, 1 - half)
    send_raw(0, half)

    slot = me % 2
    keeper = me // 2
    small = [
        (obs_weights.at[0], weights_in),
        (pair_source.at[0], source_in),
        (pair_taper.at[0], choice_in),
    ]

    def small_remote(i, side):
        return pltpu.make_async_remote_copy(
            src_ref=small[i][0],
            dst_ref=small[i][1].at[slot],
            send_sem=small_send.at[i, side],
            recv_sem=small_recv.at[i, slot],
            device_id=(device_of(side, keeper), part),
            device_id_type=MESH,
        )

    def small_arrived():
        for i in range(len(small)):
            for s in range(2):
                here = small[i][1].at[s]
                pltpu.make_async_copy(here, here, small_recv.at[i, s]).wait()

    for copy in own_copies:
        copy.wait()
    values_copy.wait()
    others = values.at[:, pl.ds(0, (n - 1) * owned)]
    pltpu.make_async_copy(others, others, values_recv).wait()

    def innovate(p, _):
        here = columns(p)
        innov[:, here] = (
            values[:, here] + own_noise[:, here].astype(jnp.float32) - own_state[:, here].astype(jnp.float32)
        ).astype(jnp.bfloat16)
        return 0

    lax.fori_loop(0, places, innovate, 0)

    def send_innov(k, _):
        where = lax.rem(place + places - k, places)
        pltpu.make_async_remote_copy(
            src_ref=innov.at[:, columns(where)],
            dst_ref=inn.at[seat_rows],
            send_sem=inn_send,
            recv_sem=inn_recv,
            device_id=(device_of(half, where), part),
            device_id_type=MESH,
        ).start()
        return 0

    lax.fori_loop(1, places, send_innov, 0)
    inn_copy = pltpu.make_async_copy(innov.at[:, mine], inn.at[seat_rows], local_sem.at[variables + 4])
    inn_copy.start()

    send_guests()
    for side in range(2):
        @pl.when(device_of(side, keeper) != me)
        def _():
            for i in range(len(small)):
                small_remote(i, side).start()

        @pl.when(device_of(side, keeper) == me)
        def _():
            for i in range(len(small)):
                pltpu.make_async_copy(small[i][0], small[i][1].at[slot], small_recv.at[i, slot]).start()

    def send_rest():
        for v in range(1, variables):
            send_raw(v, 1 - half)
            send_raw(v, half)

    @pl.when(jnp.logical_not(leads))
    def _():
        send_rest()


    taper_copy.wait()

    def flip(k, _):
        taper_t[k] = taper_in[k].T * (1.0 / (members - 1))
        return 0

    lax.fori_loop(0, tapers.shape[0], flip, 0)

    remote_rows = pl.ds(0, (n - 1) * rows)

    def arrived(v):
        raw_local[v].wait()
        block = rin.at[v, remote_rows]
        pltpu.make_async_copy(block, block, in_recv.at[v]).wait()

    def centered(array):
        numbers = array.astype(jnp.float32)
        center = jnp.sum(numbers, axis=0, keepdims=True) * (1.0 / members)
        return (numbers - center).astype(jnp.bfloat16)

    def block_of(b):
        return pl.ds(pl.multiple_of(b * size, size), size)

    def exchange(index, before, after, sources, targets):
        left = pltpu.make_async_remote_copy(
            src_ref=sources[0],
            dst_ref=targets[1],
            send_sem=halo_send.at[index, 0],
            recv_sem=halo_recv.at[index, 0],
            device_id=(device_of(half, jnp.maximum(place - 1, 0)), part),
            device_id_type=MESH,
        )
        right = pltpu.make_async_remote_copy(
            src_ref=sources[1],
            dst_ref=targets[0],
            send_sem=halo_send.at[index, 1],
            recv_sem=halo_recv.at[index, 1],
            device_id=(device_of(half, jnp.minimum(place + 1, places - 1)), part),
            device_id_type=MESH,
        )

        def start(side):
            @pl.when((before, after)[side])
            def _():
                (left, right)[side].start()

        def landed(side):
            @pl.when((before, after)[side])
            def _():
                (left, right)[side].wait_send()
                (right, left)[side].wait_recv()

        return start, landed

    at_start, at_landed = exchange(
        0,
        jnp.logical_and(leads, jnp.logical_and(place > 0, place != high)),
        jnp.logical_and(leads, jnp.logical_and(place < places - 1, place != low)),
        (at_left.at[pl.ds(RADIUS, RADIUS)], at_right.at[pl.ds(per - RADIUS, RADIUS)]),
        (at_left.at[pl.ds(0, RADIUS)], at_right.at[pl.ds(per, RADIUS)]),
    )
    w_start, w_landed = exchange(
        1,
        place > 0,
        place < places - 1,
        (win_w.at[pl.ds(RADIUS, RADIUS)], win_w.at[pl.ds(per, RADIUS)]),
        (win_w.at[pl.ds(0, RADIUS)], win_w.at[pl.ds(RADIUS + per, RADIUS)]),
    )

    @pl.when(leads)
    def _():
        arrived(0)

        def prepare(b, _):
            first = centered(rin[0, :, block_of(b)])
            anom[0, :, block_of(b)] = first
            flipped = first.T
            at_left[RADIUS + b] = flipped
            at_right[b] = flipped
            return 0

        lax.fori_loop(0, RADIUS, prepare, 0)
        at_start(0)
        lax.fori_loop(RADIUS, per, prepare, 0)
        at_start(1)
        send_rest()

    small_arrived()
    inn_copy.wait()
    others_rows = inn.at[pl.ds(0, (places - 1) * rows)]
    pltpu.make_async_copy(others_rows, others_rows, inn_recv).wait()

    def weigh(b, _):
        win_w[RADIUS + b] = lax.dot_general(
            inn[:, block_of(b)],
            weights_in[b // blocks, b % blocks],
            (((1,), (1,)), ((), ())),
            preferred_element_type=jnp.float32,
        ).astype(jnp.bfloat16)
        return 0

    lax.fori_loop(0, per, weigh, 0)
    for side in range(2):
        w_start(side)


    @pl.when(is_guest)
    def _():
        pltpu.make_async_copy(guest_in.at[my_rows], guest_in.at[my_rows], guest_local).wait()
        block = guest_in.at[remote_rows]
        pltpu.make_async_copy(block, block, guest_recv).wait()
        for b in range(RADIUS):
            flipped = centered(guest_in[:, b * size : (b + 1) * size]).T

            @pl.when(place == low)
            def _():
                at_right[per + b] = flipped

            @pl.when(place == high)
            def _():
                at_left[b] = flipped

    base = place * per - RADIUS

    def near(b, j):
        return jnp.clip(source_in[b // blocks, b % blocks, j] - base, 0, win_w.shape[0] - 1)

    turned = place // (places // 4) % 2
    bound = per // 2

    def source_block(side, b, j):
        if side:
            return at_right[jnp.clip(near(b, j) - RADIUS, 0, at_right.shape[0] - 1)]
        return at_left[jnp.minimum(near(b, j), at_left.shape[0] - 1)]

    def loc_copy(v, b):
        return pltpu.make_async_remote_copy(
            src_ref=loc.at[v, b],
            dst_ref=loc.at[v, b],
            send_sem=loc_send.at[v, b],
            recv_sem=loc_recv.at[v, b],
            device_id=(device_of(1 - half, place), part),
            device_id_type=MESH,
        )

    def localize(v, side):
        def step(b, _):
            for j in range(pairs):
                covariance = jnp.dot(
                    source_block(side, b, j),
                    anom[v, :, block_of(b)],
                    preferred_element_type=jnp.float32,
                )
                loc[v, b, pl.ds(j * size, size), :] = (
                    covariance * taper_t[choice_in[b // blocks, b % blocks, j]]
                ).astype(jnp.bfloat16)
            loc_copy(v, b).start()
            return 0

        lax.fori_loop(side * bound, side * bound + bound, step, 0)

    def center_all(v):
        def step(b, _):
            anom[v, :, block_of(b)] = centered(rin[v, :, block_of(b)])
            return 0

        lax.fori_loop(0, per, step, 0)

    def answer(v, b):
        weights = jnp.concatenate([win_w[near(b, j)] for j in range(pairs)], axis=1)
        increment = jnp.dot(weights, loc[v, b], preferred_element_type=jnp.float32)
        outbuf[v, :, block_of(b)] = increment.astype(jnp.bfloat16)
        there = pl.ds(pl.multiple_of(place * width + b * size, size), size)

        def give(k, _):
            peer = lax.rem(seat + k, places)
            theirs = pl.ds(pl.multiple_of(peer * rows, rows), rows)
            pltpu.make_async_remote_copy(
                src_ref=outbuf.at[v, theirs, block_of(b)],
                dst_ref=out.at[v, :, there],
                send_sem=out_send,
                recv_sem=out_recv,
                device_id=(half * places + peer, part),
                device_id_type=MESH,
            ).start()
            return 0

        lax.fori_loop(1, places, give, 0)
        pltpu.make_async_copy(outbuf.at[v, seat_rows, block_of(b)], out.at[v, :, there], keep_sem).start()

    def answers(v):
        def step(b, _):
            answer(v, b)
            return 0

        lax.fori_loop(0, per, step, 0)

    early = max(variables - 1, 1)

    @pl.when(leads)
    def _():
        def stage(k, _):
            for side in range(2):
                @pl.when((k + turned) % 2 == side)
                def _():
                    at_landed(side)
                    localize(0, side)

                    @pl.when(k == 0)
                    def _():
                        for v in range(1, early):
                            arrived(v)
                            center_all(v)

                    for v in range(1, early):
                        localize(v, side)

            return 0

        lax.fori_loop(0, 2, stage, 0)
        for v in range(early, variables):
            arrived(v)
            center_all(v)
            for side in range(2):
                localize(v, side)

    w_landed(0)
    w_landed(1)

    @pl.when(leads)
    def _():
        for v in range(variables):
            answers(v)

    @pl.when(jnp.logical_not(leads))
    def _():
        for v in range(variables):
            block = rin.at[v, pl.ds(0, places * rows)]
            pltpu.make_async_copy(block, block, in_send.at[v]).wait()

    @pl.when(jnp.logical_not(leads))
    def _():
        def reply(v, b):
            loc_copy(v, b).wait_recv()
            answer(v, b)

        def stage(k, _):
            for v in range(early):
                def step(i, _, v=v):
                    reply(v, (k + turned) % 2 * bound + i)
                    return 0

                lax.fori_loop(0, bound, step, 0)
            return 0

        lax.fori_loop(0, 2, stage, 0)
        for v in range(early, variables):
            def step(b, _, v=v):
                reply(v, b)
                return 0

            lax.fori_loop(0, per, step, 0)

    @pl.when(leads)
    def _():
        for v in range(variables):
            def sent(b, _, v=v):
                loc_copy(v, b).wait_send()
                return 0

            lax.fori_loop(0, per, sent, 0)

    for v in range(variables):
        @pl.when(leads)
        def _():
            block = rin.at[v, pl.ds(0, (places - 1) * rows)]
            pltpu.make_async_copy(block, block, in_send.at[v]).wait()


    @pl.when(is_guest)
    def _():
        block = guest_in.at[pl.ds(0, rows)]
        pltpu.make_async_copy(block, block, guest_send).wait()

    @pl.when(jnp.logical_not(is_guest))
    def _():
        block = guest_in.at[pl.ds(0, 2 * rows)]
        pltpu.make_async_copy(block, block, guest_send).wait()

    for side in range(2):
        @pl.when(device_of(side, keeper) != me)
        def _():
            for i in range(len(small)):
                small_remote(i, side).wait_send()

    pltpu.make_async_copy(others, others, values_send).wait()
    pltpu.make_async_copy(others_rows, others_rows, inn_send).wait()
    kept = outbuf.at[:, pl.ds(0, rows), :]
    pltpu.make_async_copy(kept, kept, keep_sem).wait()
    block = outbuf.at[:, pl.ds(0, (places - 1) * rows), :]
    pltpu.make_async_copy(block, block, out_send).wait()
    pltpu.make_async_copy(block, block, out_recv).wait()


def finish(state, increment):
    parts = 6
    depth, rows, cells = state.shape
    width = cells * depth // parts

    def body(given, added, out, held, went):
        def piece(i):
            per = parts // depth
            return i // per, slice(None), pl.ds((i % per) * width, width)

        writes = [pltpu.make_async_copy(held.at[piece(i)], out.at[piece(i)], went.at[i]) for i in range(parts)]
        for i in range(parts):
            held[piece(i)] = (
                given[piece(i)].astype(jnp.float32) + added[piece(i)].astype(jnp.float32)
            ).astype(jnp.bfloat16)
            writes[i].start()
        for copy in writes:
            copy.wait()

    near = pl.BlockSpec(memory_space=pltpu.VMEM)
    return pl.pallas_call(
        body,
        out_shape=jax.ShapeDtypeStruct(state.shape, state.dtype),
        in_specs=[near, near],
        out_specs=pl.BlockSpec(memory_space=pltpu.HBM),
        scratch_shapes=[
            pltpu.VMEM(state.shape, state.dtype),
            pltpu.SemaphoreType.DMA((parts,)),
        ],
        compiler_params=pltpu.CompilerParams(vmem_limit_bytes=8 * 1024 * 1024),
    )(state, increment)


def on_device(n, state, obs_noise, obs_values, obs_weights, tapers, pair_source, pair_taper):
    variables, rows, cells = state.shape
    members = rows * n
    places = n // 2
    width = cells // places
    blocks, size = obs_weights.shape[1], obs_weights.shape[2]
    per = width // size
    pairs = pair_source.shape[2]
    window = per + 2 * RADIUS
    anywhere = pl.BlockSpec(memory_space=pl.ANY)
    increment = pl.pallas_call(
        functools.partial(kernel, n),
        out_shape=jax.ShapeDtypeStruct(state.shape, state.dtype),
        in_specs=[pl.BlockSpec(memory_space=pltpu.HBM)] * 7,
        out_specs=anywhere,
        scratch_shapes=[
            pltpu.VMEM((rows, cells), jnp.bfloat16),
            pltpu.VMEM((rows, cells), jnp.bfloat16),
            pltpu.VMEM((rows, cells), jnp.bfloat16),
            pltpu.VMEM((1, cells), jnp.float32),
            pltpu.VMEM((variables, members, width), jnp.bfloat16),
            pltpu.VMEM((members, RADIUS * size), jnp.bfloat16),
            pltpu.VMEM((places * rows, width), jnp.bfloat16),
            pltpu.VMEM((variables, members, width), jnp.bfloat16),
            pltpu.VMEM((per + RADIUS, size, members), jnp.bfloat16),
            pltpu.VMEM((per + RADIUS, size, members), jnp.bfloat16),
            pltpu.VMEM((window, places * rows, size), jnp.bfloat16),
            pltpu.VMEM((variables, per, pairs * size, size), jnp.bfloat16),
            pltpu.VMEM(tapers.shape, jnp.float32),
            pltpu.VMEM(tapers.shape, jnp.float32),
            pltpu.VMEM((variables, places * rows, width), jnp.bfloat16),
            pltpu.VMEM((2, blocks, size, size), jnp.bfloat16),
            pltpu.SMEM((2, blocks, pairs), jnp.int32),
            pltpu.SMEM((2, blocks, pairs), jnp.int32),
            pltpu.SemaphoreType.DMA((variables + 5,)),
            pltpu.SemaphoreType.DMA,
            pltpu.SemaphoreType.DMA,
            pltpu.SemaphoreType.DMA((variables,)),
            pltpu.SemaphoreType.DMA((variables,)),
            pltpu.SemaphoreType.DMA,
            pltpu.SemaphoreType.DMA,
            pltpu.SemaphoreType.DMA,
            pltpu.SemaphoreType.DMA,
            pltpu.SemaphoreType.DMA,
            pltpu.SemaphoreType.DMA((3, 2)),
            pltpu.SemaphoreType.DMA((3, 2)),
            pltpu.SemaphoreType.DMA((2, 2)),
            pltpu.SemaphoreType.DMA((2, 2)),
            pltpu.SemaphoreType.DMA((variables, per)),
            pltpu.SemaphoreType.DMA((variables, per)),
            pltpu.SemaphoreType.DMA,
            pltpu.SemaphoreType.DMA,
            pltpu.SemaphoreType.DMA,
        ],
        compiler_params=pltpu.CompilerParams(
            collective_id=0, has_side_effects=True, vmem_limit_bytes=24 * 1024 * 1024
        ),
    )(*[pltpu.with_memory_space_constraint(x, pltpu.HBM) for x in (state, obs_noise, obs_values, obs_weights, tapers, pair_source, pair_taper)])
    return finish(state, increment)


def solution(mesh):
    placed = (
        P(None, "mem", "patch"),
        P("mem", "patch"),
        P("patch", "mem"),
        P("patch", "mem", None, None),
        P(),
        P("patch", "mem", None),
        P("patch", "mem", None),
    )
    return jax.shard_map(
        functools.partial(on_device, mesh.shape["mem"]),
        mesh=mesh,
        in_specs=placed,
        out_specs=P(None, "mem", "patch"),
        check_vma=False,
    )
```

```python
import functools

import jax
import jax.numpy as jnp
from jax import lax
from jax.experimental import pallas as pl
from jax.experimental.pallas import tpu as pltpu
from jax.sharding import PartitionSpec as P

RADIUS = 2
MESH = pl.DeviceIdType.MESH


def seat_of(place, part, places):
    span = places // 4
    leg, step = place // span, place % span
    level = (leg + 1) // 2 % 2
    step = step + (leg % 2) * (span - 1 - 2 * step)
    spot = leg // 2 * span + step
    spot = spot + (part % 2) * (2 * span - 1 - 2 * spot)
    return level * 2 * span + spot


def place_of(seat, part, places):
    span = places // 4
    level, spot = seat // (2 * span), seat % (2 * span)
    spot = spot + (part % 2) * (2 * span - 1 - 2 * spot)
    side, step = spot // span, spot % span
    leg = level + side * (3 - 2 * level)
    step = step + (leg % 2) * (span - 1 - 2 * step)
    return leg * span + step


def kernel(
    n,
    state, noise, obs_values, obs_weights, tapers, pair_source, pair_taper,
    out,
    own_state, own_noise, innov, values, rin, guest_in, inn, anom, at_left, at_right, win_w, loc, taper_in, taper_t, outbuf,
    weights_in, source_in, choice_in,
    local_sem, values_send, values_recv, in_send, in_recv, guest_send, guest_recv, guest_local,
    inn_send, inn_recv, small_send, small_recv, halo_send, halo_recv, loc_send, loc_recv,
    out_send, out_recv, keep_sem,
):
    me = lax.axis_index("mem")
    part = lax.axis_index("patch")
    variables, rows, cells = state.shape
    places = n // 2
    leads_each = places // 2
    width = cells // places
    owned = cells // n
    blocks, size = obs_weights.shape[1], obs_weights.shape[2]
    per = width // size
    pairs = pair_source.shape[2]
    members = n * rows
    half, seat = me // places, me % places
    place = place_of(seat, part, places)
    leads = place // leads_each == half
    low, high = leads_each - 1, leads_each
    is_guest = jnp.logical_and(leads, jnp.logical_or(place == low, place == high))
    edge = RADIUS * size

    def device_of(side, where):
        return side * places + seat_of(where, part, places)

    def lead_of(where):
        return device_of(where // leads_each, where)

    def columns(where):
        return pl.ds(pl.multiple_of(where * width, width), width)

    barrier = pltpu.get_barrier_semaphore()

    def greet(k, _):
        peer = lax.rem(me + k, n)
        pl.semaphore_signal(barrier, inc=1, device_id=(peer, part), device_id_type=MESH)
        return 0

    lax.fori_loop(1, n, greet, 0)

    my_rows = pl.ds(pl.multiple_of(me * rows, rows), rows)
    seat_rows = pl.ds(pl.multiple_of(seat * rows, rows), rows)
    mine = columns(place)

    own_copies = [
        pltpu.make_async_copy(state.at[0], own_state, local_sem.at[variables]),
        pltpu.make_async_copy(noise, own_noise, local_sem.at[variables + 1]),
    ]
    for copy in own_copies:
        copy.start()
    taper_copy = pltpu.make_async_copy(tapers, taper_in, local_sem.at[variables + 2])
    taper_copy.start()
    my_values = values.at[:, pl.ds(pl.multiple_of(me * owned, owned), owned)]
    values_copy = pltpu.make_async_copy(obs_values, my_values, local_sem.at[variables + 3])
    values_copy.start()

    raw_local = [
        pltpu.make_async_copy(state.at[v, :, mine], rin.at[v, my_rows], local_sem.at[v]) for v in range(variables)
    ]

    @pl.when(leads)
    def _():
        for copy in raw_local:
            copy.start()

    pl.semaphore_wait(barrier, n - 1)

    def send_values(k, _):
        pltpu.make_async_remote_copy(
            src_ref=obs_values,
            dst_ref=my_values,
            send_sem=values_send,
            recv_sem=values_recv,
            device_id=(lax.rem(me + k, n), part),
            device_id_type=MESH,
        ).start()
        return 0

    lax.fori_loop(1, n, send_values, 0)

    def send_raw(v, side):
        def send(k, _):
            where = side * leads_each + lax.rem(seat + seat // leads_each * (leads_each // 2) + k, leads_each)
            peer = lead_of(where)

            @pl.when(peer != me)
            def _():
                pltpu.make_async_remote_copy(
                    src_ref=state.at[v, :, columns(where)],
                    dst_ref=rin.at[v, my_rows],
                    send_sem=in_send.at[v],
                    recv_sem=in_recv.at[v],
                    device_id=(peer, part),
                    device_id_type=MESH,
                ).start()

            return 0

        lax.fori_loop(0, leads_each, send, 0)

    def edge_of(host):
        start = high * width if host == low else high * width - edge
        return state.at[0, :, pl.ds(start, edge)]

    def send_guests():
        for host in (low, high):
            peer = lead_of(host)

            @pl.when(peer != me)
            def _():
                pltpu.make_async_remote_copy(
                    src_ref=edge_of(host),
                    dst_ref=guest_in.at[my_rows],
                    send_sem=guest_send,
                    recv_sem=guest_recv,
                    device_id=(peer, part),
                    device_id_type=MESH,
                ).start()

            @pl.when(peer == me)
            def _():
                pltpu.make_async_copy(edge_of(host), guest_in.at[my_rows], guest_local).start()

    send_raw(0, 1 - half)
    send_raw(0, half)

    slot = me % 2
    keeper = me // 2
    small = [
        (obs_weights.at[0], weights_in),
        (pair_source.at[0], source_in),
        (pair_taper.at[0], choice_in),
    ]

    def small_remote(i, side):
        return pltpu.make_async_remote_copy(
            src_ref=small[i][0],
            dst_ref=small[i][1].at[slot],
            send_sem=small_send.at[i, side],
            recv_sem=small_recv.at[i, slot],
            device_id=(device_of(side, keeper), part),
            device_id_type=MESH,
        )

    def small_arrived():
        for i in range(len(small)):
            for s in range(2):
                here = small[i][1].at[s]
                pltpu.make_async_copy(here, here, small_recv.at[i, s]).wait()

    for copy in own_copies:
        copy.wait()
    values_copy.wait()
    others = values.at[:, pl.ds(0, (n - 1) * owned)]
    pltpu.make_async_copy(others, others, values_recv).wait()

    def innovate(p, _):
        here = columns(p)
        innov[:, here] = (
            values[:, here] + own_noise[:, here].astype(jnp.float32) - own_state[:, here].astype(jnp.float32)
        ).astype(jnp.bfloat16)
        return 0

    lax.fori_loop(0, places, innovate, 0)

    def send_innov(k, _):
        where = lax.rem(place + lax.rem(k + places // 2 - 2, places - 1) + 1, places)
        pltpu.make_async_remote_copy(
            src_ref=innov.at[:, columns(where)],
            dst_ref=inn.at[seat_rows],
            send_sem=inn_send,
            recv_sem=inn_recv,
            device_id=(device_of(half, where), part),
            device_id_type=MESH,
        ).start()
        return 0

    lax.fori_loop(1, places, send_innov, 0)
    inn_copy = pltpu.make_async_copy(innov.at[:, mine], inn.at[seat_rows], local_sem.at[variables + 4])
    inn_copy.start()

    send_guests()
    for side in range(2):
        @pl.when(device_of(side, keeper) != me)
        def _():
            for i in range(len(small)):
                small_remote(i, side).start()

        @pl.when(device_of(side, keeper) == me)
        def _():
            for i in range(len(small)):
                pltpu.make_async_copy(small[i][0], small[i][1].at[slot], small_recv.at[i, slot]).start()

    def send_rest():
        for v in range(1, variables):
            send_raw(v, 1 - half)
            send_raw(v, half)

    @pl.when(jnp.logical_not(leads))
    def _():
        send_rest()


    taper_copy.wait()

    def flip(k, _):
        taper_t[k] = taper_in[k].T * (1.0 / (members - 1))
        return 0

    lax.fori_loop(0, tapers.shape[0], flip, 0)

    remote_rows = pl.ds(0, (n - 1) * rows)

    def arrived(v):
        raw_local[v].wait()
        block = rin.at[v, remote_rows]
        pltpu.make_async_copy(block, block, in_recv.at[v]).wait()

    def centered(array):
        numbers = array.astype(jnp.float32)
        center = jnp.sum(numbers, axis=0, keepdims=True) * (1.0 / members)
        return (numbers - center).astype(jnp.bfloat16)

    def block_of(b):
        return pl.ds(pl.multiple_of(b * size, size), size)

    def exchange(index, before, after, sources, targets):
        left = pltpu.make_async_remote_copy(
            src_ref=sources[0],
            dst_ref=targets[1],
            send_sem=halo_send.at[index, 0],
            recv_sem=halo_recv.at[index, 0],
            device_id=(device_of(half, jnp.maximum(place - 1, 0)), part),
            device_id_type=MESH,
        )
        right = pltpu.make_async_remote_copy(
            src_ref=sources[1],
            dst_ref=targets[0],
            send_sem=halo_send.at[index, 1],
            recv_sem=halo_recv.at[index, 1],
            device_id=(device_of(half, jnp.minimum(place + 1, places - 1)), part),
            device_id_type=MESH,
        )

        def start(side):
            @pl.when((before, after)[side])
            def _():
                (left, right)[side].start()

        def landed(side):
            @pl.when((before, after)[side])
            def _():
                (left, right)[side].wait_send()
                (right, left)[side].wait_recv()

        return start, landed

    at_start, at_landed = exchange(
        0,
        jnp.logical_and(leads, jnp.logical_and(place > 0, place != high)),
        jnp.logical_and(leads, jnp.logical_and(place < places - 1, place != low)),
        (at_left.at[pl.ds(RADIUS, RADIUS)], at_right.at[pl.ds(per - RADIUS, RADIUS)]),
        (at_left.at[pl.ds(0, RADIUS)], at_right.at[pl.ds(per, RADIUS)]),
    )
    w_start, w_landed = exchange(
        1,
        place > 0,
        place < places - 1,
        (win_w.at[pl.ds(RADIUS, RADIUS)], win_w.at[pl.ds(per, RADIUS)]),
        (win_w.at[pl.ds(0, RADIUS)], win_w.at[pl.ds(RADIUS + per, RADIUS)]),
    )

    @pl.when(leads)
    def _():
        arrived(0)

        def prepare(b, _):
            first = centered(rin[0, :, block_of(b)])
            anom[0, :, block_of(b)] = first
            flipped = first.T
            at_left[RADIUS + b] = flipped
            at_right[b] = flipped
            return 0

        lax.fori_loop(0, RADIUS, prepare, 0)
        at_start(0)
        lax.fori_loop(RADIUS, per, prepare, 0)
        at_start(1)
        send_rest()

    small_arrived()
    inn_copy.wait()
    others_rows = inn.at[pl.ds(0, (places - 1) * rows)]
    pltpu.make_async_copy(others_rows, others_rows, inn_recv).wait()

    def weigh(b, _):
        win_w[RADIUS + b] = lax.dot_general(
            inn[:, block_of(b)],
            weights_in[b // blocks, b % blocks],
            (((1,), (1,)), ((), ())),
            preferred_element_type=jnp.float32,
        ).astype(jnp.bfloat16)
        return 0

    lax.fori_loop(0, per, weigh, 0)
    for side in range(2):
        w_start(side)


    @pl.when(is_guest)
    def _():
        pltpu.make_async_copy(guest_in.at[my_rows], guest_in.at[my_rows], guest_local).wait()
        block = guest_in.at[remote_rows]
        pltpu.make_async_copy(block, block, guest_recv).wait()
        for b in range(RADIUS):
            flipped = centered(guest_in[:, b * size : (b + 1) * size]).T

            @pl.when(place == low)
            def _():
                at_right[per + b] = flipped

            @pl.when(place == high)
            def _():
                at_left[b] = flipped

    base = place * per - RADIUS

    def near(b, j):
        return jnp.clip(source_in[b // blocks, b % blocks, j] - base, 0, win_w.shape[0] - 1)

    turned = place // (places // 4) % 2
    bound = per // 2

    def source_block(side, b, j):
        if side:
            return at_right[jnp.clip(near(b, j) - RADIUS, 0, at_right.shape[0] - 1)]
        return at_left[jnp.minimum(near(b, j), at_left.shape[0] - 1)]

    def loc_copy(v, b):
        return pltpu.make_async_remote_copy(
            src_ref=loc.at[v, b],
            dst_ref=loc.at[v, b],
            send_sem=loc_send.at[v, b],
            recv_sem=loc_recv.at[v, b],
            device_id=(device_of(1 - half, place), part),
            device_id_type=MESH,
        )

    def localize(v, side):
        def step(b, _):
            for j in range(pairs):
                covariance = jnp.dot(
                    source_block(side, b, j),
                    anom[v, :, block_of(b)],
                    preferred_element_type=jnp.float32,
                )
                loc[v, b, pl.ds(j * size, size), :] = (
                    covariance * taper_t[choice_in[b // blocks, b % blocks, j]]
                ).astype(jnp.bfloat16)
            loc_copy(v, b).start()
            return 0

        lax.fori_loop(side * bound, side * bound + bound, step, 0)

    def center_all(v):
        def step(b, _):
            anom[v, :, block_of(b)] = centered(rin[v, :, block_of(b)])
            return 0

        lax.fori_loop(0, per, step, 0)

    def answer(v, b):
        weights = jnp.concatenate([win_w[near(b, j)] for j in range(pairs)], axis=1)
        increment = jnp.dot(weights, loc[v, b], preferred_element_type=jnp.float32)
        outbuf[v, :, block_of(b)] = increment.astype(jnp.bfloat16)
        there = pl.ds(pl.multiple_of(place * width + b * size, size), size)

        def give(k, _):
            peer = lax.rem(seat + k, places)
            theirs = pl.ds(pl.multiple_of(peer * rows, rows), rows)
            pltpu.make_async_remote_copy(
                src_ref=outbuf.at[v, theirs, block_of(b)],
                dst_ref=out.at[v, :, there],
                send_sem=out_send,
                recv_sem=out_recv,
                device_id=(half * places + peer, part),
                device_id_type=MESH,
            ).start()
            return 0

        lax.fori_loop(1, places, give, 0)
        pltpu.make_async_copy(outbuf.at[v, seat_rows, block_of(b)], out.at[v, :, there], keep_sem).start()

    def answers(v):
        def step(b, _):
            answer(v, b)
            return 0

        lax.fori_loop(0, per, step, 0)

    early = max(variables - 1, 1)

    @pl.when(leads)
    def _():
        def stage(k, _):
            for side in range(2):
                @pl.when((k + turned) % 2 == side)
                def _():
                    at_landed(side)
                    localize(0, side)

                    @pl.when(k == 0)
                    def _():
                        for v in range(1, early):
                            arrived(v)
                            center_all(v)

                    for v in range(1, early):
                        localize(v, side)

            return 0

        lax.fori_loop(0, 2, stage, 0)
        for v in range(early, variables):
            arrived(v)
            center_all(v)
            for side in range(2):
                localize(v, side)

    w_landed(0)
    w_landed(1)

    @pl.when(leads)
    def _():
        for v in range(variables):
            answers(v)

    @pl.when(jnp.logical_not(leads))
    def _():
        for v in range(variables):
            block = rin.at[v, pl.ds(0, places * rows)]
            pltpu.make_async_copy(block, block, in_send.at[v]).wait()

    @pl.when(jnp.logical_not(leads))
    def _():
        def reply(v, b):
            loc_copy(v, b).wait_recv()
            answer(v, b)

        def stage(k, _):
            for v in range(early):
                def step(i, _, v=v):
                    reply(v, (k + turned) % 2 * bound + i)
                    return 0

                lax.fori_loop(0, bound, step, 0)
            return 0

        lax.fori_loop(0, 2, stage, 0)
        for v in range(early, variables):
            def step(b, _, v=v):
                reply(v, b)
                return 0

            lax.fori_loop(0, per, step, 0)

    @pl.when(leads)
    def _():
        for v in range(variables):
            def sent(b, _, v=v):
                loc_copy(v, b).wait_send()
                return 0

            lax.fori_loop(0, per, sent, 0)

    for v in range(variables):
        @pl.when(leads)
        def _():
            block = rin.at[v, pl.ds(0, (places - 1) * rows)]
            pltpu.make_async_copy(block, block, in_send.at[v]).wait()


    @pl.when(is_guest)
    def _():
        block = guest_in.at[pl.ds(0, rows)]
        pltpu.make_async_copy(block, block, guest_send).wait()

    @pl.when(jnp.logical_not(is_guest))
    def _():
        block = guest_in.at[pl.ds(0, 2 * rows)]
        pltpu.make_async_copy(block, block, guest_send).wait()

    for side in range(2):
        @pl.when(device_of(side, keeper) != me)
        def _():
            for i in range(len(small)):
                small_remote(i, side).wait_send()

    pltpu.make_async_copy(others, others, values_send).wait()
    pltpu.make_async_copy(others_rows, others_rows, inn_send).wait()
    kept = outbuf.at[:, pl.ds(0, rows), :]
    pltpu.make_async_copy(kept, kept, keep_sem).wait()
    block = outbuf.at[:, pl.ds(0, (places - 1) * rows), :]
    pltpu.make_async_copy(block, block, out_send).wait()
    pltpu.make_async_copy(block, block, out_recv).wait()


def finish(state, increment):
    parts = 6
    depth, rows, cells = state.shape
    width = cells * depth // parts

    def body(given, added, out, held, went):
        def piece(i):
            per = parts // depth
            return i // per, slice(None), pl.ds((i % per) * width, width)

        writes = [pltpu.make_async_copy(held.at[piece(i)], out.at[piece(i)], went.at[i]) for i in range(parts)]
        for i in range(parts):
            held[piece(i)] = (
                given[piece(i)].astype(jnp.float32) + added[piece(i)].astype(jnp.float32)
            ).astype(jnp.bfloat16)
            writes[i].start()
        for copy in writes:
            copy.wait()

    near = pl.BlockSpec(memory_space=pltpu.VMEM)
    return pl.pallas_call(
        body,
        out_shape=jax.ShapeDtypeStruct(state.shape, state.dtype),
        in_specs=[near, near],
        out_specs=pl.BlockSpec(memory_space=pltpu.HBM),
        scratch_shapes=[
            pltpu.VMEM(state.shape, state.dtype),
            pltpu.SemaphoreType.DMA((parts,)),
        ],
        compiler_params=pltpu.CompilerParams(vmem_limit_bytes=8 * 1024 * 1024),
    )(state, increment)


def on_device(n, state, obs_noise, obs_values, obs_weights, tapers, pair_source, pair_taper):
    variables, rows, cells = state.shape
    members = rows * n
    places = n // 2
    width = cells // places
    blocks, size = obs_weights.shape[1], obs_weights.shape[2]
    per = width // size
    pairs = pair_source.shape[2]
    window = per + 2 * RADIUS
    anywhere = pl.BlockSpec(memory_space=pl.ANY)
    increment = pl.pallas_call(
        functools.partial(kernel, n),
        out_shape=jax.ShapeDtypeStruct(state.shape, state.dtype),
        in_specs=[pl.BlockSpec(memory_space=pltpu.HBM)] * 7,
        out_specs=anywhere,
        scratch_shapes=[
            pltpu.VMEM((rows, cells), jnp.bfloat16),
            pltpu.VMEM((rows, cells), jnp.bfloat16),
            pltpu.VMEM((rows, cells), jnp.bfloat16),
            pltpu.VMEM((1, cells), jnp.float32),
            pltpu.VMEM((variables, members, width), jnp.bfloat16),
            pltpu.VMEM((members, RADIUS * size), jnp.bfloat16),
            pltpu.VMEM((places * rows, width), jnp.bfloat16),
            pltpu.VMEM((variables, members, width), jnp.bfloat16),
            pltpu.VMEM((per + RADIUS, size, members), jnp.bfloat16),
            pltpu.VMEM((per + RADIUS, size, members), jnp.bfloat16),
            pltpu.VMEM((window, places * rows, size), jnp.bfloat16),
            pltpu.VMEM((variables, per, pairs * size, size), jnp.bfloat16),
            pltpu.VMEM(tapers.shape, jnp.float32),
            pltpu.VMEM(tapers.shape, jnp.float32),
            pltpu.VMEM((variables, places * rows, width), jnp.bfloat16),
            pltpu.VMEM((2, blocks, size, size), jnp.bfloat16),
            pltpu.SMEM((2, blocks, pairs), jnp.int32),
            pltpu.SMEM((2, blocks, pairs), jnp.int32),
            pltpu.SemaphoreType.DMA((variables + 5,)),
            pltpu.SemaphoreType.DMA,
            pltpu.SemaphoreType.DMA,
            pltpu.SemaphoreType.DMA((variables,)),
            pltpu.SemaphoreType.DMA((variables,)),
            pltpu.SemaphoreType.DMA,
            pltpu.SemaphoreType.DMA,
            pltpu.SemaphoreType.DMA,
            pltpu.SemaphoreType.DMA,
            pltpu.SemaphoreType.DMA,
            pltpu.SemaphoreType.DMA((3, 2)),
            pltpu.SemaphoreType.DMA((3, 2)),
            pltpu.SemaphoreType.DMA((2, 2)),
            pltpu.SemaphoreType.DMA((2, 2)),
            pltpu.SemaphoreType.DMA((variables, per)),
            pltpu.SemaphoreType.DMA((variables, per)),
            pltpu.SemaphoreType.DMA,
            pltpu.SemaphoreType.DMA,
            pltpu.SemaphoreType.DMA,
        ],
        compiler_params=pltpu.CompilerParams(
            collective_id=0, has_side_effects=True, vmem_limit_bytes=24 * 1024 * 1024
        ),
    )(*[pltpu.with_memory_space_constraint(x, pltpu.HBM) for x in (state, obs_noise, obs_values, obs_weights, tapers, pair_source, pair_taper)])
    return finish(state, increment)


def solution(mesh):
    placed = (
        P(None, "mem", "patch"),
        P("mem", "patch"),
        P("patch", "mem"),
        P("patch", "mem", None, None),
        P(),
        P("patch", "mem", None),
        P("patch", "mem", None),
    )
    return jax.shard_map(
        functools.partial(on_device, mesh.shape["mem"]),
        mesh=mesh,
        in_specs=placed,
        out_specs=P(None, "mem", "patch"),
        check_vma=False,
    )
```
